256 devices in a mesh: dp: 16 (over z, x_lo), tensor: 16 (over y, x_hi, core).
Axes of the slice: x: 4 (x_hi: 2, x_lo: 2; x = x_hi * 2 + x_lo), y: 4, z: 8, core: 2. Of those that a mesh axis runs over, the one named last changes fastest.
Arguments:
- activations: bfloat16 [8192, 32768], P('tensor', 'dp'), may hold values from -6 to 6
- cotangent: bfloat16 [8192, 32768], P('tensor', 'dp'), may hold values from -6 to 6
- first_up: bfloat16 [64, 128, 128], P('tensor', 'dp'), may hold values from -0.5 to 0.5
- second_up: bfloat16 [128, 64, 256], P('tensor', 'dp'), may hold values from -0.75 to 0.75
- second_down: bfloat16 [128, 64, 256], P('tensor', 'dp'), may hold values from -0.375 to 0.375
- first_down: bfloat16 [64, 128, 128], P('tensor', 'dp'), may hold values from -0.5 to 0.5
Outputs:
- output: bfloat16 [8192, 32768], P('tensor', 'dp')
- grad_input: bfloat16 [8192, 32768], P('tensor', 'dp')
- grad_first_up: float32 [64, 128, 128], P('tensor', 'dp')
- grad_second_up: float32 [128, 64, 256], P('tensor', 'dp')
- grad_second_down: float32 [128, 64, 256], P('tensor', 'dp')
- grad_first_down: float32 [64, 128, 128], P('tensor', 'dp')
The draws below stay inside these ranges and needn't reach their ends.
All inputs are finite; a program needn't handle non-finite values.
Results may differ from the reference program's by a relative error of at most 0.007.
Values may be sent and summed in bfloat16 or wider, within the bound.
A program may use at most 128 MiB of HBM per device.

```python
import jax
import jax.numpy as jnp
from jax import lax

NB = 64
BS = 128
EXPAND = 4
TOK_DEV = 2048
D = 8192
TOKENS = 32768
N_DP = 16


def levels(stream_key, shape, cuts, low, high):
    gain, own = 1.0, jax.random.fold_in(stream_key, 6)
    for axis_at, shards_of in cuts:
        heights = jnp.exp(jax.random.uniform(jax.random.fold_in(own, axis_at), (shards_of,), jnp.float32, low / len(cuts), high / len(cuts)))
        gain = gain * jnp.repeat(heights, shape[axis_at] // shards_of).reshape([-1 if axis == axis_at else 1 for axis in range(len(shape))])
    return gain


def normal_values(stream_key, dims, spread, most, cuts=(), held_as=jnp.bfloat16):
    array = spread * jax.random.normal(stream_key, dims, jnp.float32)
    if cuts:
        array = array * levels(stream_key, dims, cuts, -0.22, 0.18)
    return jnp.clip(array, -most, most).astype(held_as)


def setup_inputs(seed: int = 0) -> dict:
    seeds = jax.random.split(jax.random.key(seed), 7)
    return {
        "activations": normal_values(seeds[0], (D, TOKENS), 1.0, 6.0, ((0, 16), (1, 16))),
        "cotangent": normal_values(seeds[1], (D, TOKENS), 1.0, 6.0, ((0, 16), (1, 16))),
        "first_up": normal_values(seeds[2], (NB, BS, BS), BS ** -0.5, 0.5, ((0, 16), (1, 16))),
        "second_up": normal_values(seeds[3], (BS, NB, EXPAND * NB), NB ** -0.5, 0.75, ((0, 16), (1, 16))),
        "second_down": normal_values(seeds[4], (BS, NB, EXPAND * NB), (EXPAND * NB) ** -0.5, 0.375, ((0, 16), (1, 16))),
        "first_down": normal_values(seeds[5], (NB, BS, BS), BS ** -0.5, 0.5, ((0, 16), (1, 16))),
    }


def gelu_value(v):
    return 0.5 * v * (1.0 + lax.erf(v * 0.7071067811865476))


def gelu_slope(v):
    return 0.5 * (1.0 + lax.erf(v * 0.7071067811865476)) + v * jnp.exp(-0.5 * v * v) * 0.3989422804014327


def product(form, left, right):
    return jnp.einsum(form, left.astype(jnp.float32), right.astype(jnp.float32))


def reference(activations, cotangent, first_up, second_up, second_down, first_down):
    blocks = activations.reshape(NB, BS, N_DP, TOK_DEV).transpose(2, 0, 1, 3)
    backs = cotangent.reshape(NB, BS, N_DP, TOK_DEV).transpose(2, 0, 1, 3)

    def one_block(carry, pieces):
        acc_r1, acc_l1, acc_l2, acc_r2 = carry
        inputs, grads_in = pieces
        section_one = product("kit,kij->kjt", inputs, first_up).astype(jnp.bfloat16)
        pre = product("kjt,jkm->jmt", section_one, second_up)
        hid = gelu_value(pre).astype(jnp.bfloat16)
        section_three = product("jmt,jkm->kjt", hid, second_down).astype(jnp.bfloat16)
        result = product("kjt,kji->kit", section_three, first_down).astype(jnp.bfloat16)
        acc_r2 = acc_r2 + product("kjt,kit->kji", section_three, grads_in)
        back_three = product("kit,kji->kjt", grads_in, first_down).astype(jnp.bfloat16)
        acc_l2 = acc_l2 + product("jmt,kjt->jkm", hid, back_three)
        back_hid = product("kjt,jkm->jmt", back_three, second_down)
        back_pre = (back_hid * gelu_slope(pre)).astype(jnp.bfloat16)
        acc_l1 = acc_l1 + product("kjt,jmt->jkm", section_one, back_pre)
        back_one = product("jmt,jkm->kjt", back_pre, second_up).astype(jnp.bfloat16)
        acc_r1 = acc_r1 + product("kit,kjt->kij", inputs, back_one)
        grad_in = product("kjt,kij->kit", back_one, first_up).astype(jnp.bfloat16)
        return (acc_r1, acc_l1, acc_l2, acc_r2), (result, grad_in)

    start = (jnp.zeros((NB, BS, BS), jnp.float32), jnp.zeros((BS, NB, EXPAND * NB), jnp.float32),
             jnp.zeros((BS, NB, EXPAND * NB), jnp.float32), jnp.zeros((NB, BS, BS), jnp.float32))
    sums, outs = lax.scan(one_block, start, (blocks, backs))
    output = outs[0].transpose(1, 2, 0, 3).reshape(D, TOKENS)
    grad_input = outs[1].transpose(1, 2, 0, 3).reshape(D, TOKENS)
    return output, grad_input, sums[0], sums[1], sums[2], sums[3]
```

```python
import jax
import jax.numpy as jnp
from jax import lax
from jax.experimental import pallas as pl
from jax.experimental.pallas import tpu as pltpu
from jax.sharding import PartitionSpec as P

BF = jnp.bfloat16
F32 = jnp.float32
N = 16
NC = 4
TC = 512
NT = (((1,), (1,)), ((), ()))
TN = (((0,), (1,)), ((), ()))


def mm(a, b):
    return jnp.dot(a, b, preferred_element_type=F32)


def mm_nt(a, b):
    return lax.dot_general(a, b, NT, preferred_element_type=F32)


def iota(shape, dim):
    return lax.broadcasted_iota(jnp.int32, shape, dim)


def each(count, body):
    lax.fori_loop(0, count, lambda i, c: (body(i), c)[1], 0)


def kernel(
    x_hbm, g_hbm, au_hbm, ad_hbm, bu_hbm, bd_hbm,
    out_hbm, gin_hbm, r1_ref, l1_ref, l2_ref, r2_ref,
    xv, gv, au, ad, bu, bd, wau, wad, wcu, wcd, wbu, wbd, wtu, wtd,
    s1s, b3s, s1r, b3r, s3s, bos, s3r, bor, hid, slope, bp, outv, ginv,
    lacc, r1acc, r2acc, lrecv, r1recv, r2recv, r2sum,
    ag_send, ag_recv, a2a_send, a2a_recv, rs_send, rs_recv, load_sem, store_sem,
):
    me_dp = lax.axis_index("dp")
    me_tn = lax.axis_index("tensor")

    def dp_peer(r):
        return (lax.rem(me_dp + r, N), me_tn)

    def tn_peer(r):
        return (me_dp, lax.rem(me_tn + r, N))

    def load(c):
        at = pl.ds(pl.multiple_of(c * TC, TC), TC)
        return (
            pltpu.make_async_copy(x_hbm.at[:, at], xv.at[c], load_sem.at[0, c]),
            pltpu.make_async_copy(g_hbm.at[:, at], gv.at[c], load_sem.at[1, c]),
        )

    def start_load(c):
        for copy in load(c):
            copy.start()

    each(NC, start_load)

    barrier = pltpu.get_barrier_semaphore()

    def greet(r):
        pl.semaphore_signal(barrier, inc=1, device_id=dp_peer(r + 1), device_id_type=pl.DeviceIdType.MESH)
        pl.semaphore_signal(barrier, inc=1, device_id=tn_peer(r + 1), device_id_type=pl.DeviceIdType.MESH)

    each(N - 1, greet)
    pl.semaphore_wait(barrier, 2 * (N - 1))

    def remote(src, dst, send, recv, peer):
        pltpu.make_async_remote_copy(
            src_ref=src, dst_ref=dst, send_sem=send, recv_sem=recv,
            device_id=peer, device_id_type=pl.DeviceIdType.MESH,
        ).start()

    def wait_bytes(ref, sem):
        pltpu.make_async_copy(ref, ref, sem).wait()

    gathers = ((au_hbm, au), (ad_hbm, ad), (bu_hbm, bu), (bd_hbm, bd))
    for n, (shard, whole) in enumerate(gathers):
        pltpu.make_async_copy(shard, whole.at[:, me_dp], ag_recv.at[n]).start()

        def gather_send(r, n=n, shard=shard, whole=whole):
            remote(shard, whole.at[:, me_dp], ag_send.at[n], ag_recv.at[n], dp_peer(r + 1))

        each(N - 1, gather_send)

    def spread(k):
        return (iota((512, 128), 0) == 4 * iota((512, 128), 1) + k).astype(BF)

    def square(ref, k):
        return ref[k].astype(F32).reshape(128, 128).astype(BF)

    wait_bytes(au, ag_recv.at[0])
    for k in range(4):
        rows = pl.ds(128 * k, 128)
        block = square(au, k)
        wau[:, rows] = mm_nt(spread(k), block).astype(BF)
        wcu[rows, :] = mm_nt(block, spread(k)).astype(BF)
    wait_bytes(ad, ag_recv.at[1])
    for k in range(4):
        rows = pl.ds(128 * k, 128)
        block = square(ad, k)
        wad[:, rows] = mm(spread(k), block).astype(BF)
        wcd[rows, :] = lax.dot_general(block, spread(k), TN, preferred_element_type=F32).astype(BF)

    def exchange_out(c, kind, src, dst):
        def one(r):
            to = lax.rem(me_tn + r + 1, N)
            remote(src.at[c, to], dst.at[c, :, me_tn], a2a_send.at[kind], a2a_recv.at[kind, c], (me_dp, to))

        each(N - 1, one)
        pltpu.make_async_copy(src.at[c, me_tn], dst.at[c, :, me_tn], a2a_recv.at[kind, c]).start()

    def exchange_back(c, kind, src, dst):
        def one(r):
            to = lax.rem(me_tn + r + 1, N)
            remote(src.at[c, :, to], dst.at[c, me_tn], a2a_send.at[kind], a2a_recv.at[kind, c], (me_dp, to))

        each(N - 1, one)
        pltpu.make_async_copy(src.at[c, :, me_tn], dst.at[c, me_tn], a2a_recv.at[kind, c]).start()

    def stage_a(c):
        copy_x, copy_g = load(c)
        copy_x.wait()
        s1s[c] = mm(wau[...], xv[c]).astype(BF).reshape(N, 2, 16, TC)
        exchange_out(c, 0, s1s, s1r)
        copy_g.wait()
        b3s[c] = mm(wad[...], gv[c]).astype(BF).reshape(N, 2, 16, TC)
        exchange_out(c, 1, b3s, b3r)

    each(NC, stage_a)

    for n, (whole, wide, tall) in enumerate(((bu, wtu, wbu), (bd, wtd, wbd))):
        wait_bytes(whole, ag_recv.at[2 + n])
        for q in range(2):
            block = whole[q].reshape(256, 256)
            flipped = block.astype(F32).T.astype(BF)
            zero = jnp.zeros_like(block)
            row_j = lax.rem(iota((256, 256), 0) // 4, 4)
            col_j = lax.rem(iota((256, 256), 1) // 4, 4)
            for b in range(4):
                wide[q, :, pl.ds(256 * b, 256)] = jnp.where(row_j == b, block, zero)
                tall[q, b] = jnp.where(col_j == b, flipped, zero)

    lacc[...] = jnp.zeros_like(lacc)
    r1acc[...] = jnp.zeros_like(r1acc)
    r2acc[...] = jnp.zeros_like(r2acc)

    def stage_b(c):
        wait_bytes(s1r.at[c], a2a_recv.at[0, c])

        def forward(q):
            moved = s1r[c, q].reshape(256, TC)

            def block(b):
                pre = mm(wbu[q, b], moved)
                half = 0.5 * (1.0 + lax.erf(pre * 0.7071067811865476))
                rows = pl.ds(pl.multiple_of(256 * b, 256), 256)
                hid[q, rows, :] = (pre * half).astype(BF)
                slope[q, rows, :] = half + pre * jnp.exp(-0.5 * pre * pre) * 0.3989422804014327

            each(4, block)
            s3s[c, q] = mm(wtd[q], hid[q]).astype(BF).reshape(N, 16, TC)

        each(2, forward)
        exchange_back(c, 2, s3s, s3r)
        wait_bytes(b3r.at[c], a2a_recv.at[1, c])

        def backward(q):
            moved = s1r[c, q].reshape(256, TC)
            back = b3r[c, q].reshape(256, TC)
            row_j = lax.rem(iota((256, 256), 0) // 4, 4)

            def block(b):
                rows = pl.ds(pl.multiple_of(256 * b, 256), 256)
                grad = (mm(wbd[q, b], back) * slope[q, rows, :]).astype(BF)
                bp[rows, :] = grad
                part_one = jnp.where(row_j == b, mm_nt(moved, grad), 0.0)
                part_two = jnp.where(row_j == b, mm_nt(back, hid[q, rows, :]), 0.0)
                lacc[0, q] += part_one.reshape(N, 16, 256)
                lacc[1, q] += part_two.reshape(N, 16, 256)

            each(4, block)
            bos[c, q] = mm(wtu[q], bp[...]).astype(BF).reshape(N, 16, TC)

        each(2, backward)
        exchange_back(c, 3, bos, bor)

    each(NC, stage_b)

    def reduce_out(n, src, dst, at):
        def one(r):
            to = lax.rem(me_dp + r + 1, N)
            remote(at(src, to), dst.at[me_dp], rs_send.at[n], rs_recv.at[n], (to, me_tn))

        each(N - 1, one)
        pltpu.make_async_copy(at(src, me_dp), dst.at[me_dp], rs_recv.at[n]).start()

    def reduce_in(n, ref):
        wait_bytes(ref, rs_recv.at[n])
        total = ref[0]
        for d in range(1, N):
            total = total + ref[d]
        return total

    reduce_out(0, lacc, lrecv, lambda ref, to: ref.at[:, :, to])

    def store(c):
        at = pl.ds(pl.multiple_of(c * TC, TC), TC)
        return (
            pltpu.make_async_copy(outv.at[c], out_hbm.at[:, at], store_sem.at[0, c]),
            pltpu.make_async_copy(ginv.at[c], gin_hbm.at[:, at], store_sem.at[1, c]),
        )

    def stage_c_out(c):
        wait_bytes(s3r.at[c], a2a_recv.at[2, c])
        moved = s3r[c].reshape(512, TC)
        outv[c] = mm(wcd[...], moved).astype(BF)
        store(c)[0].start()
        row_k = lax.rem(iota((512, 128), 0), 4)
        for p in range(2):
            part = mm_nt(moved, gv[c, pl.ds(256 * p, 256), :])
            part = jnp.where(row_k == 2 * p, part[:, :128], jnp.where(row_k == 2 * p + 1, part[:, 128:], 0.0))
            r2acc[...] += part.reshape(N, 32, 128)

    def stage_c_in(c):
        wait_bytes(bor.at[c], a2a_recv.at[3, c])
        moved = bor[c].reshape(512, TC)
        col_k = lax.rem(iota((128, 512), 1), 4)
        for p in range(2):
            part = mm_nt(xv[c, pl.ds(256 * p, 256), :], moved)
            part = jnp.where(col_k == 2 * p, part[:128], jnp.where(col_k == 2 * p + 1, part[128:], 0.0))
            r1acc[...] += part.reshape(N, 8, 512)
        ginv[c] = mm(wcu[...], moved).astype(BF)
        store(c)[1].start()

    def stage_c(c):
        stage_c_out(c)

        @pl.when(c == NC - 1)
        def _():
            reduce_out(1, r2acc, r2recv, lambda ref, to: ref.at[to])

        stage_c_in(c)

    each(NC, stage_c)
    reduce_out(2, r1acc, r1recv, lambda ref, to: ref.at[to])

    total = reduce_in(0, lrecv)
    l1_ref[...] = total[0]
    l2_ref[...] = total[1]
    r2sum[...] = reduce_in(1, r2recv)
    for k in range(4):
        r2_ref[k] = r2sum[pl.ds(k, 8, stride=4), :]
    total = reduce_in(2, r1recv)
    for k in range(4):
        r1_ref[k] = jnp.dot(total, spread(k).astype(F32), preferred_element_type=F32, precision=lax.Precision.HIGHEST)

    def finish(c):
        for copy in store(c):
            copy.wait()

    each(NC, finish)
    for n, (_, whole) in enumerate(gathers):
        wait_bytes(whole.at[:, pl.ds(0, N - 1)], ag_send.at[n])
    wait_bytes(s1s.at[:, pl.ds(0, N - 1)], a2a_send.at[0])
    wait_bytes(b3s.at[:, pl.ds(0, N - 1)], a2a_send.at[1])
    wait_bytes(s3s.at[:, :, pl.ds(0, N - 1)], a2a_send.at[2])
    wait_bytes(bos.at[:, :, pl.ds(0, N - 1)], a2a_send.at[3])
    wait_bytes(lrecv.at[pl.ds(0, N - 1)], rs_send.at[0])
    wait_bytes(r2recv.at[pl.ds(0, N - 1)], rs_send.at[1])
    wait_bytes(r1recv.at[pl.ds(0, N - 1)], rs_send.at[2])


def local(activations, cotangent, first_up, second_up, second_down, first_down):
    any_spec = pl.BlockSpec(memory_space=pl.ANY)
    vmem = pl.BlockSpec(memory_space=pltpu.VMEM)
    scratch = [
        pltpu.VMEM((NC, 512, TC), BF),
        pltpu.VMEM((NC, 512, TC), BF),
        pltpu.VMEM((4, N, 8, 128), BF),
        pltpu.VMEM((4, N, 8, 128), BF),
        pltpu.VMEM((2, N, 16, 256), BF),
        pltpu.VMEM((2, N, 16, 256), BF),
        pltpu.VMEM((512, 512), BF),
        pltpu.VMEM((512, 512), BF),
        pltpu.VMEM((512, 512), BF),
        pltpu.VMEM((512, 512), BF),
        pltpu.VMEM((2, 4, 256, 256), BF),
        pltpu.VMEM((2, 4, 256, 256), BF),
        pltpu.VMEM((2, 256, 1024), BF),
        pltpu.VMEM((2, 256, 1024), BF),
        pltpu.VMEM((NC, N, 2, 16, TC), BF),
        pltpu.VMEM((NC, N, 2, 16, TC), BF),
        pltpu.VMEM((NC, 2, N, 16, TC), BF),
        pltpu.VMEM((NC, 2, N, 16, TC), BF),
        pltpu.VMEM((NC, 2, N, 16, TC), BF),
        pltpu.VMEM((NC, 2, N, 16, TC), BF),
        pltpu.VMEM((NC, N, 2, 16, TC), BF),
        pltpu.VMEM((NC, N, 2, 16, TC), BF),
        pltpu.VMEM((2, 1024, TC), BF),
        pltpu.VMEM((2, 1024, TC), F32),
        pltpu.VMEM((1024, TC), BF),
        pltpu.VMEM((NC, 512, TC), BF),
        pltpu.VMEM((NC, 512, TC), BF),
        pltpu.VMEM((2, 2, N, 16, 256), F32),
        pltpu.VMEM((N, 8, 512), F32),
        pltpu.VMEM((N, 32, 128), F32),
        pltpu.VMEM((N, 2, 2, 16, 256), F32),
        pltpu.VMEM((N, 8, 512), F32),
        pltpu.VMEM((N, 32, 128), F32),
        pltpu.VMEM((32, 128), F32),
        pltpu.SemaphoreType.DMA((4,)),
        pltpu.SemaphoreType.DMA((4,)),
        pltpu.SemaphoreType.DMA((4,)),
        pltpu.SemaphoreType.DMA((4, NC)),
        pltpu.SemaphoreType.DMA((3,)),
        pltpu.SemaphoreType.DMA((3,)),
        pltpu.SemaphoreType.DMA((2, NC)),
        pltpu.SemaphoreType.DMA((2, NC)),
    ]
    out, gin, r1, l1, l2, r2 = pl.pallas_call(
        kernel,
        name="monarch_layer",
        out_shape=(
            jax.ShapeDtypeStruct((512, 2048), BF),
            jax.ShapeDtypeStruct((512, 2048), BF),
            jax.ShapeDtypeStruct((4, 8, 128), F32),
            jax.ShapeDtypeStruct((2, 16, 256), F32),
            jax.ShapeDtypeStruct((2, 16, 256), F32),
            jax.ShapeDtypeStruct((4, 8, 128), F32),
        ),
        in_specs=[any_spec] * 6,
        out_specs=(any_spec, any_spec, vmem, vmem, vmem, vmem),
        scratch_shapes=scratch,
        compiler_params=pltpu.CompilerParams(
            collective_id=0, has_side_effects=True, vmem_limit_bytes=60 * 1024 * 1024
        ),
    )(
        activations, cotangent, first_up, first_down,
        second_up.reshape(2, 16, 256), second_down.reshape(2, 16, 256),
    )
    return out, gin, r1, l1.reshape(8, 4, 256), l2.reshape(8, 4, 256), r2


def solution(mesh):
    spec = (P("tensor", "dp"),) * 2 + (P("tensor", "dp", None),) * 4
    return jax.shard_map(local, mesh=mesh, in_specs=spec, out_specs=spec, check_vma=False)
```

```python
import jax
import jax.numpy as jnp
from jax import lax
from jax.experimental import pallas as pl
from jax.experimental.pallas import tpu as pltpu
from jax.sharding import PartitionSpec as P

BF = jnp.bfloat16
F32 = jnp.float32
N = 16
NZ = 8
NC = 4
TC = 512
B_SHAPE = (2, 4, 4, 256)
L_SHAPE = (8, 4, 256)
NT = (((1,), (1,)), ((), ()))
TN = (((0,), (1,)), ((), ()))


def mm(a, b):
    return jnp.dot(a, b, preferred_element_type=F32)


def mm_nt(a, b):
    return lax.dot_general(a, b, NT, preferred_element_type=F32)


def iota(shape, dim):
    return lax.broadcasted_iota(jnp.int32, shape, dim)


def each(count, body):
    lax.fori_loop(0, count, lambda i, c: (body(i), c)[1], 0)


def kernel(
    x_hbm, g_hbm, au_hbm, ad_hbm, bu_hbm, bd_hbm,
    out_hbm, gin_hbm, r1_ref, l1_ref, l2_ref, r2_ref,
    xv, gv, au, ad, bu, bd, wau, wad, wcu, wcd, wbu, wbd, wtu, wtd,
    s1s, b3s, s1r, b3r, s3s, bos, s3r, bor, hid, slope, bp, outv, ginv,
    lacc, r1acc, r2acc, lrecv, r1recv, r2recv, lsum, r2sum, lpair, r2pair, r2rows,
    ag_send, ag_recv, pair_recv, a2a_send, a2a_recv, rs_send, rs_recv, half_send, half_recv,
    load_sem, store_sem,
):
    me_dp = lax.axis_index("dp")
    me_tn = lax.axis_index("tensor")
    me_z = me_dp // 2
    me_xl = lax.rem(me_dp, 2)
    pair = 2 * me_z + 1 - me_xl

    def load(c):
        at = pl.ds(pl.multiple_of(c * TC, TC), TC)
        return (
            pltpu.make_async_copy(x_hbm.at[:, at], xv.at[c], load_sem.at[0, c]),
            pltpu.make_async_copy(g_hbm.at[:, at], gv.at[c], load_sem.at[1, c]),
        )

    barrier = pltpu.get_barrier_semaphore()

    def greet(r):
        for peer in ((lax.rem(me_dp + r + 1, N), me_tn), (me_dp, lax.rem(me_tn + r + 1, N))):
            pl.semaphore_signal(barrier, inc=1, device_id=peer, device_id_type=pl.DeviceIdType.MESH)

    each(N - 1, greet)

    def start_load(c):
        copy_x, copy_g = load(c)
        copy_x.start()
        copy_g.start()

    each(NC, start_load)
    pl.semaphore_wait(barrier, 2 * (N - 1))

    def remote(src, dst, send, recv, peer):
        pltpu.make_async_remote_copy(
            src_ref=src, dst_ref=dst, send_sem=send, recv_sem=recv,
            device_id=peer, device_id_type=pl.DeviceIdType.MESH,
        ).start()

    def wait_bytes(ref, sem):
        pltpu.make_async_copy(ref, ref, sem).wait()

    first = ((au_hbm, au), (ad_hbm, ad))
    for n, (shard, whole) in enumerate(first):
        def gather_send(r, n=n, shard=shard, whole=whole):
            remote(shard, whole.at[:, me_dp], ag_send.at[n], ag_recv.at[n], (lax.rem(me_dp + r + 1, N), me_tn))

        each(N - 1, gather_send)
        pltpu.make_async_copy(shard, whole.at[:, me_dp], ag_recv.at[n]).start()

    second = ((bu_hbm, bu), (bd_hbm, bd))
    for n, (shard, whole) in enumerate(second):
        remote(shard, whole.at[:, me_dp], ag_send.at[2 + n], pair_recv.at[n], (pair, me_tn))

        def along_z(r, n=n, shard=shard, whole=whole):
            to = 2 * lax.rem(me_z + r + 1, NZ) + me_xl
            remote(shard, whole.at[:, me_dp], ag_send.at[2 + n], ag_recv.at[2 + n], (to, me_tn))

        each(NZ - 1, along_z)
        pltpu.make_async_copy(shard, whole.at[:, me_dp], ag_recv.at[2 + n]).start()

    def pass_on():
        for n, (_, whole) in enumerate(second):
            wait_bytes(whole.at[:, pair], pair_recv.at[n])

            def along_z(r, n=n, whole=whole):
                to = 2 * lax.rem(me_z + r + 1, NZ) + me_xl
                remote(whole.at[:, pair], whole.at[:, pair], ag_send.at[2 + n], ag_recv.at[2 + n], (to, me_tn))

            each(NZ - 1, along_z)

    def spread(k):
        row = iota((512, 128), 0)
        j = 8 * lax.rem(row // 16, N) + 4 * (row // 256) + lax.rem(row // 4, 4)
        return jnp.logical_and(lax.rem(row, 4) == k, iota((512, 128), 1) == j).astype(BF)

    def square(ref, k):
        return ref[k].astype(F32).reshape(128, 128).astype(BF)

    def exchange(c, kind, src, dst):
        def one(r):
            to = lax.rem(me_tn + r + 1, N)
            remote(src.at[c, :, to], dst.at[c, :, me_tn], a2a_send.at[kind], a2a_recv.at[kind, c], (me_dp, to))

        each(N - 1, one)
        pltpu.make_async_copy(src.at[c, :, me_tn], dst.at[c, :, me_tn], a2a_recv.at[kind, c]).start()

    def exchange_half(c, q, src, dst):
        def one(r):
            to = lax.rem(me_tn + r + 1, N)
            remote(src.at[c, q, to], dst.at[c, q, me_tn], a2a_send.at[3], a2a_recv.at[3 + q, c], (me_dp, to))

        each(N - 1, one)
        pltpu.make_async_copy(src.at[c, q, me_tn], dst.at[c, q, me_tn], a2a_recv.at[3 + q, c]).start()

    def stage_a_up(c):
        load(c)[0].wait()
        s1s[c] = mm(wau[...], xv[c]).astype(BF).reshape(2, N, 16, TC)
        exchange(c, 0, s1s, s1r)

    def stage_a_down(c):
        load(c)[1].wait()
        b3s[c] = mm(wad[...], gv[c]).astype(BF).reshape(2, N, 16, TC)
        exchange(c, 1, b3s, b3r)

    wait_bytes(au, ag_recv.at[0])
    for k in range(4):
        wau[:, pl.ds(128 * k, 128)] = mm_nt(spread(k), square(au, k)).astype(BF)
    stage_a_up(0)
    wait_bytes(ad, ag_recv.at[1])
    for k in range(4):
        wad[:, pl.ds(128 * k, 128)] = mm(spread(k), square(ad, k)).astype(BF)
    stage_a_down(0)
    pass_on()

    def stage_a(c):
        stage_a_up(c + 1)
        stage_a_down(c + 1)

    each(NC - 1, stage_a)
    for k in range(4):
        rows = pl.ds(128 * k, 128)
        wcu[rows, :] = mm_nt(square(au, k), spread(k)).astype(BF)
        wcd[rows, :] = lax.dot_general(square(ad, k), spread(k), TN, preferred_element_type=F32).astype(BF)

    for n, (whole, wide, tall) in enumerate(((bu, wtu, wbu), (bd, wtd, wbd))):
        wait_bytes(whole.at[:, pl.ds(0, N - 1)], ag_recv.at[2 + n])
        for q in range(2):
            block = whole[q].reshape(256, 256)
            flipped = block.astype(F32).T.astype(BF)
            zero = jnp.zeros_like(block)
            row_j = lax.rem(iota((256, 256), 0) // 4, 4)
            col_j = lax.rem(iota((256, 256), 1) // 4, 4)
            for b in range(4):
                wide[q, :, pl.ds(256 * b, 256)] = jnp.where(row_j == b, block, zero)
                tall[q, b] = jnp.where(col_j == b, flipped, zero)

    lacc[...] = jnp.zeros_like(lacc)
    r1acc[...] = jnp.zeros_like(r1acc)
    r2acc[...] = jnp.zeros_like(r2acc)

    def stage_b(c):
        wait_bytes(s1r.at[c], a2a_recv.at[0, c])

        def forward(q):
            moved = s1r[c, q].reshape(256, TC)

            def block(b):
                pre = mm(wbu[q, b], moved)
                half = 0.5 * (1.0 + lax.erf(pre * 0.7071067811865476))
                rows = pl.ds(pl.multiple_of(256 * b, 256), 256)
                hid[q, rows, :] = (pre * half).astype(BF)
                slope[q, rows, :] = half + pre * jnp.exp(-0.5 * pre * pre) * 0.3989422804014327

            each(4, block)
            s3s[c, q] = mm(wtd[q], hid[q]).astype(BF).reshape(N, 16, TC)

        each(2, forward)
        exchange(c, 2, s3s, s3r)
        wait_bytes(b3r.at[c], a2a_recv.at[1, c])

        def backward(q):
            moved = s1r[c, q].reshape(256, TC)
            back = b3r[c, q].reshape(256, TC)
            row_j = lax.rem(iota((256, 256), 0) // 4, 4)

            def slopes(b):
                rows = pl.ds(pl.multiple_of(256 * b, 256), 256)
                bp[rows, :] = (mm(wbd[q, b], back) * slope[q, rows, :]).astype(BF)

            each(4, slopes)
            bos[c, q] = mm(wtu[q], bp[...]).astype(BF).reshape(N, 16, TC)
            exchange_half(c, q, bos, bor)

            def sums(b):
                rows = pl.ds(pl.multiple_of(256 * b, 256), 256)
                part_one = jnp.where(row_j == b, mm_nt(moved, bp[rows, :]), 0.0)
                part_two = jnp.where(row_j == b, mm_nt(back, hid[q, rows, :]), 0.0)
                lacc[q] += part_one.reshape(NZ, 2, 16, 256)
                lacc[2 + q] += part_two.reshape(NZ, 2, 16, 256)

            each(4, sums)

        each(2, backward)

    each(NC, stage_b)

    def sum_z_out(n, acc, recv):
        def one(r):
            to = lax.rem(me_z + r + 1, NZ)
            remote(acc.at[:, to], recv.at[me_z], rs_send.at[n], rs_recv.at[n], (2 * to + me_xl, me_tn))

        each(NZ - 1, one)
        pltpu.make_async_copy(acc.at[:, me_z], recv.at[me_z], rs_recv.at[n]).start()

    def sum_z_in(n, recv, sums, pair_ref):
        wait_bytes(recv, rs_recv.at[n])
        for h in range(2):
            total = recv[0, :, h]
            for d in range(1, NZ):
                total = total + recv[d, :, h]
            sums[h] = total
        remote(sums.at[1 - me_xl], pair_ref, half_send.at[n], half_recv.at[n], (pair, me_tn))

    def sum_pair(n, sums, pair_ref):
        wait_bytes(pair_ref, half_recv.at[n])
        return sums[me_xl] + pair_ref[...]

    def sum_out(n, src, dst):
        def one(r):
            to = lax.rem(me_dp + r + 1, N)
            remote(src.at[n, to], dst.at[n, me_dp], rs_send.at[2 + n], rs_recv.at[2 + n], (to, me_tn))

        each(N - 1, one)
        pltpu.make_async_copy(src.at[n, me_dp], dst.at[n, me_dp], rs_recv.at[2 + n]).start()

    sum_z_out(0, lacc, lrecv)

    def store(c):
        at = pl.ds(pl.multiple_of(c * TC, TC), TC)
        return (
            pltpu.make_async_copy(outv.at[c], out_hbm.at[:, at], store_sem.at[0, c]),
            pltpu.make_async_copy(ginv.at[c], gin_hbm.at[:, at], store_sem.at[1, c]),
        )

    def stage_c_out(c):
        wait_bytes(s3r.at[c], a2a_recv.at[2, c])
        moved = s3r[c].reshape(512, TC)
        row_k = lax.rem(iota((512, 128), 0), 4)
        for p in range(2):
            part = mm_nt(moved, gv[c, pl.ds(256 * p, 256), :])
            part = jnp.where(row_k == 2 * p, part[:, :128], jnp.where(row_k == 2 * p + 1, part[:, 128:], 0.0))
            r2acc[...] += part.reshape(2, NZ, 2, 16, 128)

        @pl.when(c == NC - 1)
        def _():
            sum_z_out(1, r2acc, r2recv)

        outv[c] = mm(wcd[...], moved).astype(BF)
        store(c)[0].start()

    def stage_c_in(c):
        col_k = lax.rem(iota((128, 256), 1), 4)

        def half(q):
            wait_bytes(bor.at[c, q], a2a_recv.at[3 + q, c])
            moved = bor[c, q].reshape(256, TC)
            for p in range(2):
                part = mm_nt(xv[c, pl.ds(256 * p, 256), :], moved)
                part = jnp.where(col_k == 2 * p, part[:128], jnp.where(col_k == 2 * p + 1, part[128:], 0.0))
                r1acc[q] += part.reshape(N, 8, 256)

            @pl.when(c == NC - 1)
            def _():
                sum_out(q, r1acc, r1recv)

        each(2, half)
        ginv[c] = mm(wcu[...], bor[c].reshape(512, TC)).astype(BF)
        store(c)[1].start()

    def stage_c(c):
        @pl.when(c == NC - 1)
        def _():
            sum_z_in(0, lrecv, lsum, lpair)

        stage_c_out(c)
        stage_c_in(c)

    each(NC, stage_c)

    sum_z_in(1, r2recv, r2sum, r2pair)
    total = sum_pair(0, lsum, lpair)
    l1_ref[...] = total[:2].reshape(L_SHAPE)
    l2_ref[...] = total[2:].reshape(L_SHAPE)
    half_sums = []
    for q in range(2):
        wait_bytes(r1recv.at[q], rs_recv.at[2 + q])
        total = r1recv[q, 0]
        for d in range(1, N):
            total = total + r1recv[q, d]
        half_sums.append(total)
    total = jnp.concatenate(half_sums, axis=1)
    for k in range(4):
        r1_ref[k] = jnp.dot(total, spread(k).astype(F32), preferred_element_type=F32, precision=lax.Precision.HIGHEST)
    r2rows[...] = sum_pair(1, r2sum, r2pair).reshape(32, 128)
    for k in range(4):
        r2_ref[k] = r2rows[pl.ds(k, 8, stride=4), :]

    def finish(c):
        copy_out, copy_in = store(c)
        copy_out.wait()
        copy_in.wait()

    each(NC, finish)
    for n, (_, whole) in enumerate(first + second):
        wait_bytes(whole.at[:, pl.ds(0, N - 1)], ag_send.at[n])
    for n, src in enumerate((s1s, b3s, s3s, bos)):
        wait_bytes(src.at[:, :, pl.ds(0, N - 1)], a2a_send.at[n])
    wait_bytes(lrecv.at[pl.ds(0, NZ - 1)], rs_send.at[0])
    wait_bytes(r2recv.at[pl.ds(0, NZ - 1)], rs_send.at[1])
    for q in range(2):
        wait_bytes(r1recv.at[q, pl.ds(0, N - 1)], rs_send.at[2 + q])
    wait_bytes(lpair, half_send.at[0])
    wait_bytes(r2pair, half_send.at[1])


def local(activations, cotangent, first_up, second_up, second_down, first_down):
    any_spec = pl.BlockSpec(memory_space=pl.ANY)
    vmem = pl.BlockSpec(memory_space=pltpu.VMEM)
    scratch = [
        pltpu.VMEM((NC, 512, TC), BF),
        pltpu.VMEM((NC, 512, TC), BF),
        pltpu.VMEM((4, N, 8, 128), BF),
        pltpu.VMEM((4, N, 8, 128), BF),
        pltpu.VMEM((2, N) + B_SHAPE[1:], BF),
        pltpu.VMEM((2, N) + B_SHAPE[1:], BF),
        pltpu.VMEM((512, 512), BF),
        pltpu.VMEM((512, 512), BF),
        pltpu.VMEM((512, 512), BF),
        pltpu.VMEM((512, 512), BF),
        pltpu.VMEM((2, 4, 256, 256), BF),
        pltpu.VMEM((2, 4, 256, 256), BF),
        pltpu.VMEM((2, 256, 1024), BF),
        pltpu.VMEM((2, 256, 1024), BF),
        pltpu.VMEM((NC, 2, N, 16, TC), BF),
        pltpu.VMEM((NC, 2, N, 16, TC), BF),
        pltpu.VMEM((NC, 2, N, 16, TC), BF),
        pltpu.VMEM((NC, 2, N, 16, TC), BF),
        pltpu.VMEM((NC, 2, N, 16, TC), BF),
        pltpu.VMEM((NC, 2, N, 16, TC), BF),
        pltpu.VMEM((NC, 2, N, 16, TC), BF),
        pltpu.VMEM((NC, 2, N, 16, TC), BF),
        pltpu.VMEM((2, 1024, TC), BF),
        pltpu.VMEM((2, 1024, TC), F32),
        pltpu.VMEM((1024, TC), BF),
        pltpu.VMEM((NC, 512, TC), BF),
        pltpu.VMEM((NC, 512, TC), BF),
        pltpu.VMEM((4, NZ, 2, 16, 256), F32),
        pltpu.VMEM((2, N, 8, 256), F32),
        pltpu.VMEM((2, NZ, 2, 16, 128), F32),
        pltpu.VMEM((NZ, 4, 2, 16, 256), F32),
        pltpu.VMEM((2, N, 8, 256), F32),
        pltpu.VMEM((NZ, 2, 2, 16, 128), F32),
        pltpu.VMEM((2, 4, 16, 256), F32),
        pltpu.VMEM((2, 2, 16, 128), F32),
        pltpu.VMEM((4, 16, 256), F32),
        pltpu.VMEM((2, 16, 128), F32),
        pltpu.VMEM((32, 128), F32),
        pltpu.SemaphoreType.DMA((4,)),
        pltpu.SemaphoreType.DMA((4,)),
        pltpu.SemaphoreType.DMA((2,)),
        pltpu.SemaphoreType.DMA((4,)),
        pltpu.SemaphoreType.DMA((5, NC)),
        pltpu.SemaphoreType.DMA((4,)),
        pltpu.SemaphoreType.DMA((4,)),
        pltpu.SemaphoreType.DMA((2,)),
        pltpu.SemaphoreType.DMA((2,)),
        pltpu.SemaphoreType.DMA((2, NC)),
        pltpu.SemaphoreType.DMA((2, NC)),
    ]
    out, gin, r1, l1, l2, r2 = pl.pallas_call(
        kernel,
        name="monarch_layer",
        out_shape=(
            jax.ShapeDtypeStruct((512, 2048), BF),
            jax.ShapeDtypeStruct((512, 2048), BF),
            jax.ShapeDtypeStruct((4, 8, 128), F32),
            jax.ShapeDtypeStruct(L_SHAPE, F32),
            jax.ShapeDtypeStruct(L_SHAPE, F32),
            jax.ShapeDtypeStruct((4, 8, 128), F32),
        ),
        in_specs=[any_spec] * 6,
        out_specs=(any_spec, any_spec, vmem, vmem, vmem, vmem),
        scratch_shapes=scratch,
        compiler_params=pltpu.CompilerParams(
            collective_id=0, has_side_effects=True, vmem_limit_bytes=60 * 1024 * 1024
        ),
    )(
        activations, cotangent, first_up, first_down,
        second_up.reshape(B_SHAPE), second_down.reshape(B_SHAPE),
    )
    return out, gin, r1, l1.reshape(8, 4, 256), l2.reshape(8, 4, 256), r2


def solution(mesh):
    spec = (P("tensor", "dp"),) * 2 + (P("tensor", "dp", None),) * 4
    return jax.shard_map(local, mesh=mesh, in_specs=spec, out_specs=spec, check_vma=False)
```

```python
import jax
import jax.numpy as jnp
from jax import lax
from jax.experimental import pallas as pl
from jax.experimental.pallas import tpu as pltpu
from jax.sharding import PartitionSpec as P

BF = jnp.bfloat16
F32 = jnp.float32
N = 16
NZ = 8
NC = 4
TC = 512
B_SHAPE = (2, 4, 4, 256)
L_SHAPE = (8, 4, 256)
NT = (((1,), (1,)), ((), ()))
TN = (((0,), (1,)), ((), ()))


def mm(a, b):
    return jnp.dot(a, b, preferred_element_type=F32)


def mm_nt(a, b):
    return lax.dot_general(a, b, NT, preferred_element_type=F32)


def iota(shape, dim):
    return lax.broadcasted_iota(jnp.int32, shape, dim)


def each(count, body):
    lax.fori_loop(0, count, lambda i, c: (body(i), c)[1], 0)


def kernel(
    x_hbm, g_hbm, au_hbm, ad_hbm, bu_hbm, bd_hbm,
    out_hbm, gin_hbm, r1_ref, l1_ref, l2_ref, r2_ref,
    xv, gv, au, ad, bu, bd, wau, wad, wcu, wcd, wbu, wbd, wtu, wtd,
    s1s, b3s, s1r, b3r, s3s, bos, s3r, bor, hid, slope, bp, outv, ginv,
    perm, lacc, r1acc, r2acc, lrecv, r1recv, r2recv, lsum, r2sum, lpair, r2pair, r2rows,
    ag_send, ag_recv, pair_recv, a2a_send, a2a_recv, rs_send, rs_recv, half_send, half_recv,
    own_sem, load_sem, store_sem,
):
    me_dp = lax.axis_index("dp")
    me_tn = lax.axis_index("tensor")
    me_z = me_dp // 2
    me_xl = lax.rem(me_dp, 2)
    pair = 2 * me_z + 1 - me_xl

    def load(c):
        at = pl.ds(pl.multiple_of(c * TC, TC), TC)
        return (
            pltpu.make_async_copy(x_hbm.at[:, at], xv.at[c], load_sem.at[0, c]),
            pltpu.make_async_copy(g_hbm.at[:, at], gv.at[c], load_sem.at[1, c]),
        )

    barrier = pltpu.get_barrier_semaphore()

    def greet(r):
        for peer in ((lax.rem(me_dp + r + 1, N), me_tn), (me_dp, lax.rem(me_tn + r + 1, N))):
            pl.semaphore_signal(barrier, inc=1, device_id=peer, device_id_type=pl.DeviceIdType.MESH)

    each(N - 1, greet)

    def start_load(c):
        copy_x, copy_g = load(c)
        copy_x.start()
        copy_g.start()

    first = ((au_hbm, au), (ad_hbm, ad))
    second = ((bu_hbm, bu), (bd_hbm, bd))
    own = [
        pltpu.make_async_copy(shard, whole.at[:, me_dp], own_sem.at[n])
        for n, (shard, whole) in enumerate(first + second)
    ]
    for copy in own:
        copy.start()
    each(NC, start_load)

    row, col = iota((512, 512), 0), iota((512, 512), 1)
    place = 128 * lax.rem(row, 4) + 8 * lax.rem(row // 16, N) + 4 * (row // 256) + lax.rem(row // 4, 4)
    perm[...] = (place == col).astype(BF)
    for copy in own:
        copy.wait()
    pl.semaphore_wait(barrier, 2 * (N - 1))

    def remote(src, dst, send, recv, peer):
        pltpu.make_async_remote_copy(
            src_ref=src, dst_ref=dst, send_sem=send, recv_sem=recv,
            device_id=peer, device_id_type=pl.DeviceIdType.MESH,
        ).start()

    def wait_bytes(ref, sem):
        pltpu.make_async_copy(ref, ref, sem).wait()

    for n, (_, whole) in enumerate(first):
        def gather_send(r, n=n, whole=whole):
            mine = whole.at[:, me_dp]
            remote(mine, mine, ag_send.at[n], ag_recv.at[n], (lax.rem(me_dp + r + 1, N), me_tn))

        each(N - 1, gather_send)

    for n, (_, whole) in enumerate(second):
        mine = whole.at[:, me_dp]
        remote(mine, mine, ag_send.at[2 + n], pair_recv.at[n], (pair, me_tn))

        def along_z(r, n=n, whole=whole):
            mine = whole.at[:, me_dp]
            to = 2 * lax.rem(me_z + r + 1, NZ) + me_xl
            remote(mine, mine, ag_send.at[2 + n], ag_recv.at[2 + n], (to, me_tn))

        each(NZ - 1, along_z)

    def pass_on():
        for n, (_, whole) in enumerate(second):
            wait_bytes(whole.at[:, pair], pair_recv.at[n])

            def along_z(r, n=n, whole=whole):
                to = 2 * lax.rem(me_z + r + 1, NZ) + me_xl
                remote(whole.at[:, pair], whole.at[:, pair], ag_send.at[2 + n], ag_recv.at[2 + n], (to, me_tn))

            each(NZ - 1, along_z)

    def spread(k):
        return perm[:, pl.ds(128 * k, 128)]

    def square(ref, k):
        return ref[k].astype(F32).reshape(128, 128).astype(BF)

    def exchange(c, kind, src, dst):
        def one(r):
            to = lax.rem(me_tn + r + 1, N)
            remote(src.at[c, :, to], dst.at[c, :, me_tn], a2a_send.at[kind], a2a_recv.at[kind, c], (me_dp, to))

        each(N - 1, one)
        pltpu.make_async_copy(src.at[c, :, me_tn], dst.at[c, :, me_tn], a2a_recv.at[kind, c]).start()

    def exchange_half(c, q, src, dst):
        def one(r):
            to = lax.rem(me_tn + r + 1, N)
            remote(src.at[c, q, to], dst.at[c, q, me_tn], a2a_send.at[3], a2a_recv.at[3 + q, c], (me_dp, to))

        each(N - 1, one)
        pltpu.make_async_copy(src.at[c, q, me_tn], dst.at[c, q, me_tn], a2a_recv.at[3 + q, c]).start()

    def stage_a_up(c):
        load(c)[0].wait()
        s1s[c] = mm(wau[...], xv[c]).astype(BF).reshape(2, N, 16, TC)
        exchange(c, 0, s1s, s1r)

    def stage_a_down(c):
        load(c)[1].wait()
        b3s[c] = mm(wad[...], gv[c]).astype(BF).reshape(2, N, 16, TC)
        exchange(c, 1, b3s, b3r)

    wait_bytes(au.at[:, pl.ds(0, N - 1)], ag_recv.at[0])
    for k in range(4):
        wau[:, pl.ds(128 * k, 128)] = mm_nt(spread(k), square(au, k)).astype(BF)
    stage_a_up(0)
    wait_bytes(ad.at[:, pl.ds(0, N - 1)], ag_recv.at[1])
    for k in range(4):
        wad[:, pl.ds(128 * k, 128)] = mm(spread(k), square(ad, k)).astype(BF)
    stage_a_down(0)
    pass_on()

    def stage_a(c):
        stage_a_up(c + 1)
        stage_a_down(c + 1)

    each(NC - 1, stage_a)
    for k in range(4):
        rows = pl.ds(128 * k, 128)
        wcu[rows, :] = mm_nt(square(au, k), spread(k)).astype(BF)
        wcd[rows, :] = lax.dot_general(square(ad, k), spread(k), TN, preferred_element_type=F32).astype(BF)

    for n, (whole, wide, tall) in enumerate(((bu, wtu, wbu), (bd, wtd, wbd))):
        wait_bytes(whole.at[:, pl.ds(0, N - 2)], ag_recv.at[2 + n])
        for q in range(2):
            block = whole[q].reshape(256, 256)
            flipped = block.astype(F32).T.astype(BF)
            zero = jnp.zeros_like(block)
            row_j = lax.rem(iota((256, 256), 0) // 4, 4)
            col_j = lax.rem(iota((256, 256), 1) // 4, 4)
            for b in range(4):
                wide[q, :, pl.ds(256 * b, 256)] = jnp.where(row_j == b, block, zero)
                tall[q, b] = jnp.where(col_j == b, flipped, zero)

    lacc[...] = jnp.zeros_like(lacc)
    r1acc[...] = jnp.zeros_like(r1acc)
    r2acc[...] = jnp.zeros_like(r2acc)

    def stage_b(c):
        wait_bytes(s1r.at[c], a2a_recv.at[0, c])

        def forward(q):
            moved = s1r[c, q].reshape(256, TC)

            def block(b):
                pre = mm(wbu[q, b], moved)
                half = 0.5 * (1.0 + lax.erf(pre * 0.7071067811865476))
                rows = pl.ds(pl.multiple_of(256 * b, 256), 256)
                hid[q, rows, :] = (pre * half).astype(BF)
                slope[q, rows, :] = half + pre * jnp.exp(-0.5 * pre * pre) * 0.3989422804014327

            each(4, block)
            s3s[c, q] = mm(wtd[q], hid[q]).astype(BF).reshape(N, 16, TC)

        each(2, forward)
        exchange(c, 2, s3s, s3r)
        wait_bytes(b3r.at[c], a2a_recv.at[1, c])

        def backward(q):
            moved = s1r[c, q].reshape(256, TC)
            back = b3r[c, q].reshape(256, TC)
            row_j = lax.rem(iota((256, 256), 0) // 4, 4)

            def slopes(b):
                rows = pl.ds(pl.multiple_of(256 * b, 256), 256)
                bp[rows, :] = (mm(wbd[q, b], back) * slope[q, rows, :]).astype(BF)

            each(4, slopes)
            bos[c, q] = mm(wtu[q], bp[...]).astype(BF).reshape(N, 16, TC)
            exchange_half(c, q, bos, bor)

            def sums(b):
                rows = pl.ds(pl.multiple_of(256 * b, 256), 256)
                part_one = jnp.where(row_j == b, mm_nt(moved, bp[rows, :]), 0.0)
                part_two = jnp.where(row_j == b, mm_nt(back, hid[q, rows, :]), 0.0)
                lacc[q] += part_one.reshape(NZ, 2, 16, 256)
                lacc[2 + q] += part_two.reshape(NZ, 2, 16, 256)

            each(4, sums)

        each(2, backward)

    each(NC, stage_b)

    def sum_z_out(n, acc, recv):
        def one(r):
            to = lax.rem(me_z + r + 1, NZ)
            remote(acc.at[:, to], recv.at[me_z], rs_send.at[n], rs_recv.at[n], (2 * to + me_xl, me_tn))

        each(NZ - 1, one)
        pltpu.make_async_copy(acc.at[:, me_z], recv.at[me_z], rs_recv.at[n]).start()

    def sum_z_in(n, recv, sums, pair_ref):
        wait_bytes(recv, rs_recv.at[n])
        for h in range(2):
            total = recv[0, :, h]
            for d in range(1, NZ):
                total = total + recv[d, :, h]
            sums[h] = total
        remote(sums.at[1 - me_xl], pair_ref, half_send.at[n], half_recv.at[n], (pair, me_tn))

    def sum_pair(n, sums, pair_ref):
        wait_bytes(pair_ref, half_recv.at[n])
        return sums[me_xl] + pair_ref[...]

    def sum_out(n, src, dst):
        def one(r):
            to = lax.rem(me_dp + r + 1, N)
            remote(src.at[n, to], dst.at[n, me_dp], rs_send.at[2 + n], rs_recv.at[2 + n], (to, me_tn))

        each(N - 1, one)
        pltpu.make_async_copy(src.at[n, me_dp], dst.at[n, me_dp], rs_recv.at[2 + n]).start()

    sum_z_out(0, lacc, lrecv)

    def store(c):
        at = pl.ds(pl.multiple_of(c * TC, TC), TC)
        return (
            pltpu.make_async_copy(outv.at[c], out_hbm.at[:, at], store_sem.at[0, c]),
            pltpu.make_async_copy(ginv.at[c], gin_hbm.at[:, at], store_sem.at[1, c]),
        )

    def stage_c_out(c):
        wait_bytes(s3r.at[c], a2a_recv.at[2, c])
        moved = s3r[c].reshape(512, TC)
        row_k = lax.rem(iota((512, 128), 0), 4)
        for p in range(2):
            part = mm_nt(moved, gv[c, pl.ds(256 * p, 256), :])
            part = jnp.where(row_k == 2 * p, part[:, :128], jnp.where(row_k == 2 * p + 1, part[:, 128:], 0.0))
            r2acc[...] += part.reshape(2, NZ, 2, 16, 128)

        @pl.when(c == NC - 1)
        def _():
            sum_z_out(1, r2acc, r2recv)

        outv[c] = mm(wcd[...], moved).astype(BF)
        store(c)[0].start()

    def stage_c_in(c):
        col_k = lax.rem(iota((128, 256), 1), 4)

        def half(q):
            wait_bytes(bor.at[c, q], a2a_recv.at[3 + q, c])
            moved = bor[c, q].reshape(256, TC)
            for p in range(2):
                part = mm_nt(xv[c, pl.ds(256 * p, 256), :], moved)
                part = jnp.where(col_k == 2 * p, part[:128], jnp.where(col_k == 2 * p + 1, part[128:], 0.0))
                r1acc[q] += part.reshape(N, 8, 256)

            @pl.when(c == NC - 1)
            def _():
                sum_out(q, r1acc, r1recv)

        each(2, half)
        ginv[c] = mm(wcu[...], bor[c].reshape(512, TC)).astype(BF)
        store(c)[1].start()

    def stage_c(c):
        @pl.when(c == NC - 1)
        def _():
            sum_z_in(0, lrecv, lsum, lpair)

        stage_c_out(c)
        stage_c_in(c)

    each(NC, stage_c)

    sum_z_in(1, r2recv, r2sum, r2pair)
    total = sum_pair(0, lsum, lpair)
    l1_ref[...] = total[:2].reshape(L_SHAPE)
    l2_ref[...] = total[2:].reshape(L_SHAPE)
    r2rows[...] = sum_pair(1, r2sum, r2pair).reshape(32, 128)
    for k in range(4):
        r2_ref[k] = r2rows[pl.ds(k, 8, stride=4), :]

    def finish(c):
        copy_out, copy_in = store(c)
        copy_out.wait()
        copy_in.wait()

    each(NC, finish)
    for n, (_, whole) in enumerate(first + second):
        wait_bytes(whole.at[:, pl.ds(0, N - 1)], ag_send.at[n])
    for n, src in enumerate((s1s, b3s, s3s, bos)):
        wait_bytes(src.at[:, :, pl.ds(0, N - 1)], a2a_send.at[n])
    wait_bytes(lrecv.at[pl.ds(0, NZ - 1)], rs_send.at[0])
    wait_bytes(r2recv.at[pl.ds(0, NZ - 1)], rs_send.at[1])
    wait_bytes(lpair, half_send.at[0])
    wait_bytes(r2pair, half_send.at[1])

    ordered = jnp.zeros((8, 512), F32)
    for q in range(2):
        wait_bytes(r1recv.at[q], rs_recv.at[2 + q])
        total = r1recv[q, 0]
        for d in range(1, N):
            total = total + r1recv[q, d]
        high = total.astype(BF).astype(F32)
        middle = (total - high).astype(BF).astype(F32)
        parts = jnp.concatenate((high, middle, total - high - middle), axis=0).astype(BF)
        moved = mm(parts, perm[pl.ds(256 * q, 256), :])
        ordered = ordered + (moved[:8] + moved[8:16] + moved[16:])
    for k in range(4):
        r1_ref[k] = ordered[:, 128 * k : 128 * k + 128]
    for q in range(2):
        wait_bytes(r1recv.at[q, pl.ds(0, N - 1)], rs_send.at[2 + q])


def settle(*refs):
    copies = [pltpu.make_async_copy(refs[n], refs[6 + n], refs[12].at[n]) for n in range(6)]
    for copy in copies:
        copy.start()
    for copy in copies:
        copy.wait()


def local(activations, cotangent, first_up, second_up, second_down, first_down):
    any_spec = pl.BlockSpec(memory_space=pl.ANY)
    vmem = pl.BlockSpec(memory_space=pltpu.VMEM)
    hbm = pl.BlockSpec(memory_space=pltpu.HBM)
    scratch = [
        pltpu.VMEM((NC, 512, TC), BF),
        pltpu.VMEM((NC, 512, TC), BF),
        pltpu.VMEM((4, N, 8, 128), BF),
        pltpu.VMEM((4, N, 8, 128), BF),
        pltpu.VMEM((2, N) + B_SHAPE[1:], BF),
        pltpu.VMEM((2, N) + B_SHAPE[1:], BF),
        pltpu.VMEM((512, 512), BF),
        pltpu.VMEM((512, 512), BF),
        pltpu.VMEM((512, 512), BF),
        pltpu.VMEM((512, 512), BF),
        pltpu.VMEM((2, 4, 256, 256), BF),
        pltpu.VMEM((2, 4, 256, 256), BF),
        pltpu.VMEM((2, 256, 1024), BF),
        pltpu.VMEM((2, 256, 1024), BF),
        pltpu.VMEM((NC, 2, N, 16, TC), BF),
        pltpu.VMEM((NC, 2, N, 16, TC), BF),
        pltpu.VMEM((NC, 2, N, 16, TC), BF),
        pltpu.VMEM((NC, 2, N, 16, TC), BF),
        pltpu.VMEM((NC, 2, N, 16, TC), BF),
        pltpu.VMEM((NC, 2, N, 16, TC), BF),
        pltpu.VMEM((NC, 2, N, 16, TC), BF),
        pltpu.VMEM((NC, 2, N, 16, TC), BF),
        pltpu.VMEM((2, 1024, TC), BF),
        pltpu.VMEM((2, 1024, TC), F32),
        pltpu.VMEM((1024, TC), BF),
        pltpu.VMEM((NC, 512, TC), BF),
        pltpu.VMEM((NC, 512, TC), BF),
        pltpu.VMEM((512, 512), BF),
        pltpu.VMEM((4, NZ, 2, 16, 256), F32),
        pltpu.VMEM((2, N, 8, 256), F32),
        pltpu.VMEM((2, NZ, 2, 16, 128), F32),
        pltpu.VMEM((NZ, 4, 2, 16, 256), F32),
        pltpu.VMEM((2, N, 8, 256), F32),
        pltpu.VMEM((NZ, 2, 2, 16, 128), F32),
        pltpu.VMEM((2, 4, 16, 256), F32),
        pltpu.VMEM((2, 2, 16, 128), F32),
        pltpu.VMEM((4, 16, 256), F32),
        pltpu.VMEM((2, 16, 128), F32),
        pltpu.VMEM((32, 128), F32),
        pltpu.SemaphoreType.DMA((4,)),
        pltpu.SemaphoreType.DMA((4,)),
        pltpu.SemaphoreType.DMA((2,)),
        pltpu.SemaphoreType.DMA((4,)),
        pltpu.SemaphoreType.DMA((5, NC)),
        pltpu.SemaphoreType.DMA((4,)),
        pltpu.SemaphoreType.DMA((4,)),
        pltpu.SemaphoreType.DMA((2,)),
        pltpu.SemaphoreType.DMA((2,)),
        pltpu.SemaphoreType.DMA((4,)),
        pltpu.SemaphoreType.DMA((2, NC)),
        pltpu.SemaphoreType.DMA((2, NC)),
    ]
    results = pl.pallas_call(
        kernel,
        name="monarch_layer",
        out_shape=(
            jax.ShapeDtypeStruct((512, 2048), BF),
            jax.ShapeDtypeStruct((512, 2048), BF),
            jax.ShapeDtypeStruct((4, 8, 128), F32),
            jax.ShapeDtypeStruct(L_SHAPE, F32),
            jax.ShapeDtypeStruct(L_SHAPE, F32),
            jax.ShapeDtypeStruct((4, 8, 128), F32),
        ),
        in_specs=[hbm] * 6,
        out_specs=(any_spec, any_spec, vmem, vmem, vmem, vmem),
        scratch_shapes=scratch,
        compiler_params=pltpu.CompilerParams(
            collective_id=0, has_side_effects=True, vmem_limit_bytes=49 * 1024 * 1024
        ),
    )(
        *(
            pltpu.with_memory_space_constraint(value, pltpu.HBM)
            for value in (
                activations, cotangent, first_up, first_down,
                second_up.reshape(B_SHAPE), second_down.reshape(B_SHAPE),
            )
        )
    )
    return tuple(
        pl.pallas_call(
            settle,
            name="settle",
            out_shape=tuple(jax.ShapeDtypeStruct(r.shape, r.dtype) for r in results),
            in_specs=[any_spec] * 6,
            out_specs=(hbm,) * 6,
            compiler_params=pltpu.CompilerParams(vmem_limit_bytes=1024 * 1024),
            scratch_shapes=[pltpu.SemaphoreType.DMA((6,))],
        )(*results)
    )


def solution(mesh):
    spec = (P("tensor", "dp"),) * 2 + (P("tensor", "dp", None),) * 4
    return jax.shard_map(local, mesh=mesh, in_specs=spec, out_specs=spec, check_vma=False)
```

```python
import jax
import jax.numpy as jnp
from jax import lax
from jax.experimental import pallas as pl
from jax.experimental.pallas import tpu as pltpu
from jax.sharding import PartitionSpec as P

BF = jnp.bfloat16
F32 = jnp.float32
N = 16
NZ = 8
NC = 4
TC = 512
B_SHAPE = (2, 4, 4, 256)
L_SHAPE = (8, 4, 256)
NT = (((1,), (1,)), ((), ()))
TN = (((0,), (1,)), ((), ()))


def mm(a, b):
    return jnp.dot(a, b, preferred_element_type=F32)


def mm_nt(a, b):
    return lax.dot_general(a, b, NT, preferred_element_type=F32)


def iota(shape, dim):
    return lax.broadcasted_iota(jnp.int32, shape, dim)


def each(count, body):
    lax.fori_loop(0, count, lambda i, c: (body(i), c)[1], 0)


def kernel(
    x_hbm, g_hbm, au_hbm, ad_hbm, bu_hbm, bd_hbm,
    out_hbm, gin_hbm, r1_ref, l1_ref, l2_ref, r2_ref,
    xv, gv, au, ad, bu, bd, wau, wad, wcu, wcd, wbu, wbd, wtu, wtd,
    s1s, b3s, s1r, b3r, s3s, bos, s3r, bor, hid, slope, bp, outv, ginv,
    perm, lacc, r1acc, r2acc, r1out, r2out, lrecv, r1recv, r2recv, lsum, r2sum, lpair, r2pair, r2rows,
    ag_send, ag_recv, pair_recv, a2a_send, a2a_recv, rs_send, rs_recv, half_send, half_recv,
    own_sem, load_sem, store_sem,
):
    me_dp = lax.axis_index("dp")
    me_tn = lax.axis_index("tensor")
    def far_first(i, size):
        return size // 2 + ((i + 1) // 2) * (2 * lax.rem(i, 2) - 1)

    def other_dp(i):
        return lax.rem(me_dp + far_first(i, N), N)

    def other_z(i):
        return lax.rem(me_z + far_first(i, NZ), NZ)

    me_z = me_dp // 2
    me_xl = lax.rem(me_dp, 2)
    pair = 2 * me_z + 1 - me_xl

    def load(c):
        at = pl.ds(pl.multiple_of(c * TC, TC), TC)
        return (
            pltpu.make_async_copy(x_hbm.at[:, at], xv.at[c], load_sem.at[0, c]),
            pltpu.make_async_copy(g_hbm.at[:, at], gv.at[c], load_sem.at[1, c]),
        )

    barrier = pltpu.get_barrier_semaphore()

    def greet(r):
        for peer in ((lax.rem(me_dp + r + 1, N), me_tn), (me_dp, lax.rem(me_tn + r + 1, N))):
            pl.semaphore_signal(barrier, inc=1, device_id=peer, device_id_type=pl.DeviceIdType.MESH)

    each(N - 1, greet)

    def start_load(c):
        copy_x, copy_g = load(c)
        copy_x.start()
        copy_g.start()

    first = ((au_hbm, au), (ad_hbm, ad))
    second = ((bu_hbm, bu), (bd_hbm, bd))
    own = [
        pltpu.make_async_copy(shard, whole.at[:, me_dp], own_sem.at[n])
        for n, (shard, whole) in enumerate(first + second)
    ]
    for copy in own:
        copy.start()
    each(NC, start_load)

    row, col = iota((512, 512), 0), iota((512, 512), 1)
    place = 128 * lax.rem(row, 4) + 8 * lax.rem(row // 16, N) + 4 * (row // 256) + lax.rem(row // 4, 4)
    perm[...] = (place == col).astype(BF)
    for copy in own:
        copy.wait()
    pl.semaphore_wait(barrier, 2 * (N - 1))

    def remote(src, dst, send, recv, peer):
        pltpu.make_async_remote_copy(
            src_ref=src, dst_ref=dst, send_sem=send, recv_sem=recv,
            device_id=peer, device_id_type=pl.DeviceIdType.MESH,
        ).start()

    def wait_bytes(ref, sem):
        pltpu.make_async_copy(ref, ref, sem).wait()

    for n, (_, whole) in enumerate(first):
        def gather_send(r, n=n, whole=whole):
            mine = whole.at[:, me_dp]
            remote(mine, mine, ag_send.at[n], ag_recv.at[n], (other_dp(r), me_tn))

        each(N - 1, gather_send)

    for n, (_, whole) in enumerate(second):
        mine = whole.at[:, me_dp]
        remote(mine, mine, ag_send.at[2 + n], pair_recv.at[n], (pair, me_tn))

        def along_z(r, n=n, whole=whole):
            mine = whole.at[:, me_dp]
            to = 2 * other_z(r) + me_xl
            remote(mine, mine, ag_send.at[2 + n], ag_recv.at[2 + n], (to, me_tn))

        each(NZ - 1, along_z)

    def pass_on():
        for n, (_, whole) in enumerate(second):
            wait_bytes(whole.at[:, pair], pair_recv.at[n])

            def along_z(r, n=n, whole=whole):
                to = 2 * other_z(r) + me_xl
                remote(whole.at[:, pair], whole.at[:, pair], ag_send.at[2 + n], ag_recv.at[2 + n], (to, me_tn))

            each(NZ - 1, along_z)

    def spread(k):
        return perm[:, pl.ds(128 * k, 128)]

    def square(ref, k):
        return ref[k].astype(F32).reshape(128, 128).astype(BF)

    def exchange(c, kind, src, dst):
        def one(r):
            to = lax.rem(me_tn + r + 1, N)
            remote(src.at[c, :, to], dst.at[c, :, me_tn], a2a_send.at[kind], a2a_recv.at[kind, c], (me_dp, to))

        each(N - 1, one)
        pltpu.make_async_copy(src.at[c, :, me_tn], dst.at[c, :, me_tn], a2a_recv.at[kind, c]).start()

    def exchange_half(c, q, src, dst):
        def one(r):
            to = lax.rem(me_tn + r + 1, N)
            remote(src.at[c, q, to], dst.at[c, q, me_tn], a2a_send.at[3], a2a_recv.at[3 + q, c], (me_dp, to))

        each(N - 1, one)
        pltpu.make_async_copy(src.at[c, q, me_tn], dst.at[c, q, me_tn], a2a_recv.at[3 + q, c]).start()

    def stage_a_up(c):
        load(c)[0].wait()
        s1s[c] = mm(wau[...], xv[c]).astype(BF).reshape(2, N, 16, TC)
        exchange(c, 0, s1s, s1r)

    def stage_a_down(c):
        load(c)[1].wait()
        b3s[c] = mm(wad[...], gv[c]).astype(BF).reshape(2, N, 16, TC)
        exchange(c, 1, b3s, b3r)

    wait_bytes(au.at[:, pl.ds(0, N - 1)], ag_recv.at[0])
    for k in range(4):
        wau[:, pl.ds(128 * k, 128)] = mm_nt(spread(k), square(au, k)).astype(BF)
    stage_a_up(0)
    wait_bytes(ad.at[:, pl.ds(0, N - 1)], ag_recv.at[1])
    for k in range(4):
        wad[:, pl.ds(128 * k, 128)] = mm(spread(k), square(ad, k)).astype(BF)
    stage_a_down(0)
    pass_on()

    def stage_a(c):
        stage_a_up(c + 1)
        stage_a_down(c + 1)

    each(NC - 1, stage_a)
    for k in range(4):
        rows = pl.ds(128 * k, 128)
        wcu[rows, :] = mm_nt(square(au, k), spread(k)).astype(BF)
        wcd[rows, :] = lax.dot_general(square(ad, k), spread(k), TN, preferred_element_type=F32).astype(BF)

    for n, (whole, wide, tall) in enumerate(((bu, wtu, wbu), (bd, wtd, wbd))):
        wait_bytes(whole.at[:, pl.ds(0, N - 2)], ag_recv.at[2 + n])
        for q in range(2):
            block = whole[q].reshape(256, 256)
            flipped = block.astype(F32).T.astype(BF)
            zero = jnp.zeros_like(block)
            row_j = lax.rem(iota((256, 256), 0) // 4, 4)
            col_j = lax.rem(iota((256, 256), 1) // 4, 4)
            for b in range(4):
                wide[q, :, pl.ds(256 * b, 256)] = jnp.where(row_j == b, block, zero)
                tall[q, b] = jnp.where(col_j == b, flipped, zero)

    lacc[...] = jnp.zeros_like(lacc)
    r1acc[...] = jnp.zeros_like(r1acc)
    r2acc[...] = jnp.zeros_like(r2acc)

    def stage_b(c):
        wait_bytes(s1r.at[c], a2a_recv.at[0, c])

        def forward(q):
            moved = s1r[c, q].reshape(256, TC)

            def block(b):
                pre = mm(wbu[q, b], moved)
                half = 0.5 * (1.0 + lax.erf(pre * 0.7071067811865476))
                rows = pl.ds(pl.multiple_of(256 * b, 256), 256)
                hid[q, rows, :] = (pre * half).astype(BF)
                slope[q, rows, :] = half + pre * jnp.exp(-0.5 * pre * pre) * 0.3989422804014327

            each(4, block)
            s3s[c, q] = mm(wtd[q], hid[q]).astype(BF).reshape(N, 16, TC)

        each(2, forward)
        exchange(c, 2, s3s, s3r)
        wait_bytes(b3r.at[c], a2a_recv.at[1, c])

        def backward(q):
            moved = s1r[c, q].reshape(256, TC)
            back = b3r[c, q].reshape(256, TC)
            row_j = lax.rem(iota((256, 256), 0) // 4, 4)

            def slopes(b):
                rows = pl.ds(pl.multiple_of(256 * b, 256), 256)
                bp[rows, :] = (mm(wbd[q, b], back) * slope[q, rows, :]).astype(BF)

            each(4, slopes)
            bos[c, q] = mm(wtu[q], bp[...]).astype(BF).reshape(N, 16, TC)
            exchange_half(c, q, bos, bor)

            def sums(b):
                rows = pl.ds(pl.multiple_of(256 * b, 256), 256)
                part_one = jnp.where(row_j == b, mm_nt(moved, bp[rows, :]), 0.0)
                part_two = jnp.where(row_j == b, mm_nt(back, hid[q, rows, :]), 0.0)
                lacc[q] += part_one.reshape(NZ, 2, 16, 256)
                lacc[2 + q] += part_two.reshape(NZ, 2, 16, 256)

            each(4, sums)

        each(2, backward)

    each(NC, stage_b)

    def sum_z_out(n, acc, recv):
        def one(r):
            to = other_z(r)
            remote(acc.at[:, to], recv.at[me_z], rs_send.at[n], rs_recv.at[n], (2 * to + me_xl, me_tn))

        each(NZ - 1, one)
        pltpu.make_async_copy(acc.at[:, me_z], recv.at[me_z], rs_recv.at[n]).start()

    def sum_z_in(n, recv, sums):
        wait_bytes(recv, rs_recv.at[n])
        for h in range(2):
            total = recv[0, :, h].astype(F32)
            for d in range(1, NZ):
                total = total + recv[d, :, h].astype(F32)
            sums[h] = total

    def pair_out(n, sums, pair_ref):
        remote(sums.at[1 - me_xl], pair_ref, half_send.at[n], half_recv.at[n], (pair, me_tn))

    def sum_pair(n, sums, pair_ref):
        wait_bytes(pair_ref, half_recv.at[n])
        return sums[me_xl] + pair_ref[...]

    def sum_out(n, src, dst):
        def one(r):
            to = other_dp(r)
            remote(src.at[n, to], dst.at[n, me_dp], rs_send.at[2 + n], rs_recv.at[2 + n], (to, me_tn))

        each(N - 1, one)
        pltpu.make_async_copy(src.at[n, me_dp], dst.at[n, me_dp], rs_recv.at[2 + n]).start()

    sum_z_out(0, lacc, lrecv)

    def store(c):
        at = pl.ds(pl.multiple_of(c * TC, TC), TC)
        return (
            pltpu.make_async_copy(outv.at[c], out_hbm.at[:, at], store_sem.at[0, c]),
            pltpu.make_async_copy(ginv.at[c], gin_hbm.at[:, at], store_sem.at[1, c]),
        )

    def stage_c_out(c):
        wait_bytes(s3r.at[c], a2a_recv.at[2, c])
        moved = s3r[c].reshape(512, TC)
        row_k = lax.rem(iota((512, 128), 0), 4)
        for p in range(2):
            part = mm_nt(moved, gv[c, pl.ds(256 * p, 256), :])
            part = jnp.where(row_k == 2 * p, part[:, :128], jnp.where(row_k == 2 * p + 1, part[:, 128:], 0.0))
            r2acc[...] += part.reshape(2, NZ, 2, 16, 128)

        @pl.when(c == NC - 1)
        def _():
            r2out[...] = r2acc[...].astype(BF)
            sum_z_out(1, r2out, r2recv)

        outv[c] = mm(wcd[...], moved).astype(BF)
        store(c)[0].start()

    def stage_c_in(c):
        col_k = lax.rem(iota((128, 256), 1), 4)

        def half(q):
            wait_bytes(bor.at[c, q], a2a_recv.at[3 + q, c])
            moved = bor[c, q].reshape(256, TC)
            for p in range(2):
                part = mm_nt(xv[c, pl.ds(256 * p, 256), :], moved)
                part = jnp.where(col_k == 2 * p, part[:128], jnp.where(col_k == 2 * p + 1, part[128:], 0.0))
                r1acc[q] += part.reshape(N, 8, 256)

            @pl.when(c == NC - 1)
            def _():
                r1out[q] = r1acc[q].astype(BF)
                sum_out(q, r1out, r1recv)

        each(2, half)

        @pl.when(c == NC - 1)
        def _():
            pair_out(0, lsum, lpair)

        ginv[c] = mm(wcu[...], bor[c].reshape(512, TC)).astype(BF)
        store(c)[1].start()

    def stage_c(c):
        @pl.when(c == NC - 1)
        def _():
            sum_z_in(0, lrecv, lsum)

        stage_c_out(c)
        stage_c_in(c)

    each(NC, stage_c)

    sum_z_in(1, r2recv, r2sum)
    pair_out(1, r2sum, r2pair)
    total = sum_pair(0, lsum, lpair)
    l1_ref[...] = total[:2].reshape(L_SHAPE)
    l2_ref[...] = total[2:].reshape(L_SHAPE)
    r2rows[...] = sum_pair(1, r2sum, r2pair).reshape(32, 128)
    for k in range(4):
        r2_ref[k] = r2rows[pl.ds(k, 8, stride=4), :]

    def finish(c):
        copy_out, copy_in = store(c)
        copy_out.wait()
        copy_in.wait()

    each(NC, finish)
    for n, (_, whole) in enumerate(first + second):
        wait_bytes(whole.at[:, pl.ds(0, N - 1)], ag_send.at[n])
    for n, src in enumerate((s1s, b3s, s3s, bos)):
        wait_bytes(src.at[:, :, pl.ds(0, N - 1)], a2a_send.at[n])
    wait_bytes(lrecv.at[pl.ds(0, NZ - 1)], rs_send.at[0])
    wait_bytes(r2recv.at[pl.ds(0, NZ - 1)], rs_send.at[1])
    wait_bytes(lpair, half_send.at[0])
    wait_bytes(r2pair, half_send.at[1])

    ordered = jnp.zeros((8, 512), F32)
    for q in range(2):
        wait_bytes(r1recv.at[q], rs_recv.at[2 + q])
        total = r1recv[q, 0].astype(F32)
        for d in range(1, N):
            total = total + r1recv[q, d].astype(F32)
        high = total.astype(BF).astype(F32)
        middle = (total - high).astype(BF).astype(F32)
        parts = jnp.concatenate((high, middle, total - high - middle), axis=0).astype(BF)
        moved = mm(parts, perm[pl.ds(256 * q, 256), :])
        ordered = ordered + (moved[:8] + moved[8:16] + moved[16:])
    for k in range(4):
        r1_ref[k] = ordered[:, 128 * k : 128 * k + 128]
    for q in range(2):
        wait_bytes(r1recv.at[q, pl.ds(0, N - 1)], rs_send.at[2 + q])


def settle(*refs):
    copies = [pltpu.make_async_copy(refs[n], refs[6 + n], refs[12].at[n]) for n in range(6)]
    for copy in copies:
        copy.start()
    for copy in copies:
        copy.wait()


def local(activations, cotangent, first_up, second_up, second_down, first_down):
    any_spec = pl.BlockSpec(memory_space=pl.ANY)
    vmem = pl.BlockSpec(memory_space=pltpu.VMEM)
    hbm = pl.BlockSpec(memory_space=pltpu.HBM)
    scratch = [
        pltpu.VMEM((NC, 512, TC), BF),
        pltpu.VMEM((NC, 512, TC), BF),
        pltpu.VMEM((4, N, 8, 128), BF),
        pltpu.VMEM((4, N, 8, 128), BF),
        pltpu.VMEM((2, N) + B_SHAPE[1:], BF),
        pltpu.VMEM((2, N) + B_SHAPE[1:], BF),
        pltpu.VMEM((512, 512), BF),
        pltpu.VMEM((512, 512), BF),
        pltpu.VMEM((512, 512), BF),
        pltpu.VMEM((512, 512), BF),
        pltpu.VMEM((2, 4, 256, 256), BF),
        pltpu.VMEM((2, 4, 256, 256), BF),
        pltpu.VMEM((2, 256, 1024), BF),
        pltpu.VMEM((2, 256, 1024), BF),
        pltpu.VMEM((NC, 2, N, 16, TC), BF),
        pltpu.VMEM((NC, 2, N, 16, TC), BF),
        pltpu.VMEM((NC, 2, N, 16, TC), BF),
        pltpu.VMEM((NC, 2, N, 16, TC), BF),
        pltpu.VMEM((NC, 2, N, 16, TC), BF),
        pltpu.VMEM((NC, 2, N, 16, TC), BF),
        pltpu.VMEM((NC, 2, N, 16, TC), BF),
        pltpu.VMEM((NC, 2, N, 16, TC), BF),
        pltpu.VMEM((2, 1024, TC), BF),
        pltpu.VMEM((2, 1024, TC), F32),
        pltpu.VMEM((1024, TC), BF),
        pltpu.VMEM((NC, 512, TC), BF),
        pltpu.VMEM((NC, 512, TC), BF),
        pltpu.VMEM((512, 512), BF),
        pltpu.VMEM((4, NZ, 2, 16, 256), F32),
        pltpu.VMEM((2, N, 8, 256), F32),
        pltpu.VMEM((2, NZ, 2, 16, 128), F32),
        pltpu.VMEM((2, N, 8, 256), BF),
        pltpu.VMEM((2, NZ, 2, 16, 128), BF),
        pltpu.VMEM((NZ, 4, 2, 16, 256), F32),
        pltpu.VMEM((2, N, 8, 256), BF),
        pltpu.VMEM((NZ, 2, 2, 16, 128), BF),
        pltpu.VMEM((2, 4, 16, 256), F32),
        pltpu.VMEM((2, 2, 16, 128), F32),
        pltpu.VMEM((4, 16, 256), F32),
        pltpu.VMEM((2, 16, 128), F32),
        pltpu.VMEM((32, 128), F32),
        pltpu.SemaphoreType.DMA((4,)),
        pltpu.SemaphoreType.DMA((4,)),
        pltpu.SemaphoreType.DMA((2,)),
        pltpu.SemaphoreType.DMA((4,)),
        pltpu.SemaphoreType.DMA((5, NC)),
        pltpu.SemaphoreType.DMA((4,)),
        pltpu.SemaphoreType.DMA((4,)),
        pltpu.SemaphoreType.DMA((2,)),
        pltpu.SemaphoreType.DMA((2,)),
        pltpu.SemaphoreType.DMA((4,)),
        pltpu.SemaphoreType.DMA((2, NC)),
        pltpu.SemaphoreType.DMA((2, NC)),
    ]
    results = pl.pallas_call(
        kernel,
        name="monarch_layer",
        out_shape=(
            jax.ShapeDtypeStruct((512, 2048), BF),
            jax.ShapeDtypeStruct((512, 2048), BF),
            jax.ShapeDtypeStruct((4, 8, 128), F32),
            jax.ShapeDtypeStruct(L_SHAPE, F32),
            jax.ShapeDtypeStruct(L_SHAPE, F32),
            jax.ShapeDtypeStruct((4, 8, 128), F32),
        ),
        in_specs=[hbm] * 6,
        out_specs=(any_spec, any_spec, vmem, vmem, vmem, vmem),
        scratch_shapes=scratch,
        compiler_params=pltpu.CompilerParams(
            collective_id=0, has_side_effects=True, vmem_limit_bytes=49 * 1024 * 1024
        ),
    )(
        *(
            pltpu.with_memory_space_constraint(value, pltpu.HBM)
            for value in (
                activations, cotangent, first_up, first_down,
                second_up.reshape(B_SHAPE), second_down.reshape(B_SHAPE),
            )
        )
    )
    return tuple(
        pl.pallas_call(
            settle,
            name="settle",
            out_shape=tuple(jax.ShapeDtypeStruct(r.shape, r.dtype) for r in results),
            in_specs=[any_spec] * 6,
            out_specs=(hbm,) * 6,
            compiler_params=pltpu.CompilerParams(vmem_limit_bytes=1024 * 1024),
            scratch_shapes=[pltpu.SemaphoreType.DMA((6,))],
        )(*results)
    )


def solution(mesh):
    spec = (P("tensor", "dp"),) * 2 + (P("tensor", "dp", None),) * 4
    return jax.shard_map(local, mesh=mesh, in_specs=spec, out_specs=spec, check_vma=False)
```

```python
import jax
import jax.numpy as jnp
from jax import lax
from jax.experimental import pallas as pl
from jax.experimental.pallas import tpu as pltpu
from jax.sharding import PartitionSpec as P

BF = jnp.bfloat16
F32 = jnp.float32
N = 16
NZ = 8
NC = 4
TC = 512
PIECES = 4
B_SHAPE = (2, 4, 4, 256)
L_SHAPE = (8, 4, 256)
NT = (((1,), (1,)), ((), ()))
TN = (((0,), (1,)), ((), ()))


def mm(a, b):
    return jnp.dot(a, b, preferred_element_type=F32)


def mm_nt(a, b):
    return lax.dot_general(a, b, NT, preferred_element_type=F32)


def iota(shape, dim):
    return lax.broadcasted_iota(jnp.int32, shape, dim)


def each(count, body):
    lax.fori_loop(0, count, lambda i, c: (body(i), c)[1], 0)


def kernel(
    x_hbm, g_hbm, au_hbm, ad_hbm, bu_hbm, bd_hbm,
    out_hbm, gin_hbm, r1_ref, l1_ref, l2_ref, r2_ref,
    xv, gv, au, ad, bu, bd, wau, wad, wcu, wcd, wbu, wbd, wtu, wtd,
    s1s, b3s, s1r, b3r, s3s, bos, s3r, bor, hid, slope, bp,
    perm, lacc, r1acc, r2acc, r1out, lrecv, r1recv, r2recv, lsum, r2sum, lpair, r2pair, r2rows,
    ag_send, ag_recv, pair_recv, a2a_send, a2a_recv, rs_send, rs_recv, half_send, half_recv,
    own_sem, load_sem, store_sem,
):
    me_dp = lax.axis_index("dp")
    me_tn = lax.axis_index("tensor")
    def far_first(i, size):
        return size // 2 + ((i + 1) // 2) * (2 * lax.rem(i, 2) - 1)

    def other_dp(i):
        return lax.rem(me_dp + far_first(i, N), N)

    def other_z(i):
        return lax.rem(me_z + far_first(i, NZ), NZ)

    me_z = me_dp // 2
    me_xl = lax.rem(me_dp, 2)
    pair = 2 * me_z + 1 - me_xl

    def load(c):
        at = pl.ds(pl.multiple_of(c * TC, TC), TC)
        return (
            pltpu.make_async_copy(x_hbm.at[:, at], xv.at[c], load_sem.at[0, c]),
            pltpu.make_async_copy(g_hbm.at[:, at], gv.at[c], load_sem.at[1, c]),
        )

    barrier = pltpu.get_barrier_semaphore()

    def greet(r):
        for peer in ((lax.rem(me_dp + r + 1, N), me_tn), (me_dp, lax.rem(me_tn + r + 1, N))):
            pl.semaphore_signal(barrier, inc=1, device_id=peer, device_id_type=pl.DeviceIdType.MESH)

    each(N - 1, greet)

    def start_load(c):
        copy_x, copy_g = load(c)
        copy_x.start()
        copy_g.start()

    first = ((au_hbm, au), (ad_hbm, ad))
    second = ((bu_hbm, bu), (bd_hbm, bd))
    own = [
        pltpu.make_async_copy(shard, whole.at[:, me_dp], own_sem.at[n])
        for n, (shard, whole) in enumerate(first + second)
    ]
    for copy in own:
        copy.start()
    each(NC, start_load)

    row, col = iota((512, 512), 0), iota((512, 512), 1)
    place = 128 * lax.rem(row, 4) + 8 * lax.rem(row // 16, N) + 4 * (row // 256) + lax.rem(row // 4, 4)
    perm[...] = (place == col).astype(BF)
    for copy in own:
        copy.wait()
    pl.semaphore_wait(barrier, 2 * (N - 1))

    def remote(src, dst, send, recv, peer):
        pltpu.make_async_remote_copy(
            src_ref=src, dst_ref=dst, send_sem=send, recv_sem=recv,
            device_id=peer, device_id_type=pl.DeviceIdType.MESH,
        ).start()

    def wait_bytes(ref, sem):
        pltpu.make_async_copy(ref, ref, sem).wait()

    for n, (_, whole) in enumerate(first):
        def gather_send(r, n=n, whole=whole):
            mine = whole.at[:, me_dp]
            remote(mine, mine, ag_send.at[n], ag_recv.at[n], (other_dp(r), me_tn))

        each(N - 1, gather_send)

    for n, (_, whole) in enumerate(second):
        mine = whole.at[:, me_dp]
        remote(mine, mine, ag_send.at[2 + n], pair_recv.at[n], (pair, me_tn))

        def along_z(r, n=n, whole=whole):
            mine = whole.at[:, me_dp]
            to = 2 * other_z(r) + me_xl
            remote(mine, mine, ag_send.at[2 + n], ag_recv.at[2 + n], (to, me_tn))

        each(NZ - 1, along_z)

    def pass_on():
        for n, (_, whole) in enumerate(second):
            wait_bytes(whole.at[:, pair], pair_recv.at[n])

            def along_z(r, n=n, whole=whole):
                to = 2 * other_z(r) + me_xl
                remote(whole.at[:, pair], whole.at[:, pair], ag_send.at[2 + n], ag_recv.at[2 + n], (to, me_tn))

            each(NZ - 1, along_z)

    def spread(k):
        return perm[:, pl.ds(128 * k, 128)]

    def square(ref, k):
        return ref[k].astype(F32).reshape(128, 128).astype(BF)

    def exchange(c, kind, src, dst):
        def one(r):
            to = lax.rem(me_tn + r + 1, N)
            remote(src.at[c, :, to], dst.at[c, :, me_tn], a2a_send.at[kind], a2a_recv.at[kind, c], (me_dp, to))

        each(N - 1, one)
        pltpu.make_async_copy(src.at[c, :, me_tn], dst.at[c, :, me_tn], a2a_recv.at[kind, c]).start()

    def exchange_half(c, q, src, dst):
        def one(r):
            to = lax.rem(me_tn + r + 1, N)
            remote(src.at[c, q, to], dst.at[c, q, me_tn], a2a_send.at[3], a2a_recv.at[3 + q, c], (me_dp, to))

        each(N - 1, one)
        pltpu.make_async_copy(src.at[c, q, me_tn], dst.at[c, q, me_tn], a2a_recv.at[3 + q, c]).start()

    def stage_a_up(c):
        load(c)[0].wait()
        s1s[c] = mm(wau[...], xv[c]).astype(BF).reshape(2, N, 16, TC)
        exchange(c, 0, s1s, s1r)

    def stage_a_down(c):
        load(c)[1].wait()
        b3s[c] = mm(wad[...], gv[c]).astype(BF).reshape(2, N, 16, TC)
        exchange(c, 1, b3s, b3r)

    wait_bytes(au.at[:, pl.ds(0, N - 1)], ag_recv.at[0])
    for k in range(4):
        wau[:, pl.ds(128 * k, 128)] = mm_nt(spread(k), square(au, k)).astype(BF)
    stage_a_up(0)
    wait_bytes(ad.at[:, pl.ds(0, N - 1)], ag_recv.at[1])
    for k in range(4):
        wad[:, pl.ds(128 * k, 128)] = mm(spread(k), square(ad, k)).astype(BF)
    stage_a_down(0)
    pass_on()

    def stage_a(c):
        stage_a_up(c + 1)
        stage_a_down(c + 1)

    each(NC - 1, stage_a)
    for k in range(4):
        rows = pl.ds(128 * k, 128)
        wcu[rows, :] = mm_nt(square(au, k), spread(k)).astype(BF)
        wcd[rows, :] = lax.dot_general(square(ad, k), spread(k), TN, preferred_element_type=F32).astype(BF)

    for n, (whole, wide, tall) in enumerate(((bu, wtu, wbu), (bd, wtd, wbd))):
        wait_bytes(whole.at[:, pl.ds(0, N - 2)], ag_recv.at[2 + n])
        for q in range(2):
            block = whole[q].reshape(256, 256)
            flipped = block.astype(F32).T.astype(BF)
            zero = jnp.zeros_like(block)
            row_j = lax.rem(iota((256, 256), 0) // 4, 4)
            col_j = lax.rem(iota((256, 256), 1) // 4, 4)
            for b in range(4):
                wide[q, :, pl.ds(256 * b, 256)] = jnp.where(row_j == b, block, zero)
                tall[q, b] = jnp.where(col_j == b, flipped, zero)

    lacc[...] = jnp.zeros_like(lacc)
    r1acc[...] = jnp.zeros_like(r1acc)
    r2acc[...] = jnp.zeros_like(r2acc)

    def stage_b_forward(c):
        slot = lax.rem(c, 2)
        wait_bytes(s1r.at[c], a2a_recv.at[0, c])

        def forward(q):
            moved = s1r[c, q].reshape(256, TC)

            def block(b):
                pre = mm(wbu[q, b], moved)
                half = 0.5 * (1.0 + lax.erf(pre * 0.7071067811865476))
                rows = pl.ds(pl.multiple_of(256 * b, 256), 256)
                hid[slot, q, rows, :] = (pre * half).astype(BF)
                slope[slot, q, rows, :] = half + pre * jnp.exp(-0.5 * pre * pre) * 0.3989422804014327

            each(4, block)
            s3s[c, q] = mm(wtd[q], hid[slot, q]).astype(BF).reshape(N, 16, TC)

        each(2, forward)
        exchange(c, 2, s3s, s3r)

    def stage_b_backward(c):
        slot = lax.rem(c, 2)
        wait_bytes(b3r.at[c], a2a_recv.at[1, c])

        def backward(q):
            moved = s1r[c, q].reshape(256, TC)
            back = b3r[c, q].reshape(256, TC)
            row_j = lax.rem(iota((256, 256), 0) // 4, 4)

            def slopes(b):
                rows = pl.ds(pl.multiple_of(256 * b, 256), 256)
                bp[rows, :] = (mm(wbd[q, b], back) * slope[slot, q, rows, :]).astype(BF)

            each(4, slopes)
            bos[c, q] = mm(wtu[q], bp[...]).astype(BF).reshape(N, 16, TC)
            exchange_half(c, q, bos, bor)

            def sums(b):
                rows = pl.ds(pl.multiple_of(256 * b, 256), 256)
                part_one = jnp.where(row_j == b, mm_nt(moved, bp[rows, :]), 0.0)
                part_two = jnp.where(row_j == b, mm_nt(back, hid[slot, q, rows, :]), 0.0)
                lacc[q] += part_one.reshape(NZ, 2, 16, 256)
                lacc[2 + q] += part_two.reshape(NZ, 2, 16, 256)

            each(4, sums)

        each(2, backward)

    def stage_b(step):
        @pl.when(step < NC)
        def _():
            stage_b_forward(step)

        @pl.when(step < NC - 2)
        def _():
            stage_b_backward(step)

        @pl.when(step >= NC - 1)
        def _():
            stage_b_backward(step - 1)

    each(NC + 1, stage_b)

    def sum_z_out(n, acc, recv):
        def one(r):
            to = other_z(r)
            remote(acc.at[:, to], recv.at[me_z], rs_send.at[n], rs_recv.at[n], (2 * to + me_xl, me_tn))

        each(NZ - 1, one)
        pltpu.make_async_copy(acc.at[:, me_z], recv.at[me_z], rs_recv.at[n]).start()

    def sum_z_in(n, recv, sums):
        wait_bytes(recv, rs_recv.at[n])
        for h in range(2):
            total = recv[0, :, h].astype(F32)
            for d in range(1, NZ):
                total = total + recv[d, :, h].astype(F32)
            sums[h] = total

    def pair_out(n, sums, pair_ref):
        remote(sums.at[1 - me_xl], pair_ref, half_send.at[n], half_recv.at[n], (pair, me_tn))

    def sum_pair(n, sums, pair_ref):
        wait_bytes(pair_ref, half_recv.at[n])
        return sums[me_xl] + pair_ref[...]

    def sum_out(n, src, dst):
        def one(r):
            to = other_dp(r)
            remote(src.at[n, to], dst.at[n, me_dp], rs_send.at[2 + n], rs_recv.at[2 + n], (to, me_tn))

        each(N - 1, one)
        pltpu.make_async_copy(src.at[n, me_dp], dst.at[n, me_dp], rs_recv.at[2 + n]).start()

    sum_z_out(0, lacc, lrecv)

    def store(c):
        at = pl.ds(pl.multiple_of(c * TC, TC), TC)
        return (
            pltpu.make_async_copy(s3r.at[c], out_hbm.at[:, :, :, at], store_sem.at[0, c]),
            pltpu.make_async_copy(bor.at[c], gin_hbm.at[:, :, :, at], store_sem.at[1, c]),
        )

    def stage_c_out(c):
        wait_bytes(s3r.at[c], a2a_recv.at[2, c])
        moved = s3r[c].reshape(512, TC)
        row_k = lax.rem(iota((512, 128), 0), 4)
        for p in range(2):
            part = mm_nt(moved, gv[c, pl.ds(256 * p, 256), :])
            part = jnp.where(row_k == 2 * p, part[:, :128], jnp.where(row_k == 2 * p + 1, part[:, 128:], 0.0))
            r2acc[...] += part.reshape(2, NZ, 2, 16, 128)

        @pl.when(c == NC - 1)
        def _():
            sum_z_out(1, r2acc, r2recv)

        s3r[c] = mm(wcd[...], moved).astype(BF).reshape(2, N, 16, TC)
        store(c)[0].start()

    def stage_c_in(c):
        col_k = lax.rem(iota((128, 256), 1), 4)

        def half(q):
            wait_bytes(bor.at[c, q], a2a_recv.at[3 + q, c])
            moved = bor[c, q].reshape(256, TC)
            for p in range(2):
                part = mm_nt(xv[c, pl.ds(256 * p, 256), :], moved)
                part = jnp.where(col_k == 2 * p, part[:128], jnp.where(col_k == 2 * p + 1, part[128:], 0.0))
                r1acc[q] += part.reshape(N, 8, 256)

            @pl.when(c == NC - 1)
            def _():
                r1out[q] = r1acc[q].astype(BF)
                sum_out(q, r1out, r1recv)

        each(2, half)

        @pl.when(c == NC - 1)
        def _():
            pair_out(0, lsum, lpair)
            sum_z_in(1, r2recv, r2sum)
            pair_out(1, r2sum, r2pair)

        bor[c] = mm(wcu[...], bor[c].reshape(512, TC)).astype(BF).reshape(2, N, 16, TC)
        store(c)[1].start()

    def stage_c(step):
        @pl.when(step < NC)
        def _():
            stage_c_out(step)

        @pl.when(step < NC - 2)
        def _():
            stage_c_in(step)

        @pl.when(step == NC)
        def _():
            sum_z_in(0, lrecv, lsum)

        @pl.when(step >= NC - 1)
        def _():
            stage_c_in(step - 1)

    each(NC + 1, stage_c)

    total = sum_pair(0, lsum, lpair)
    l1_ref[...] = total[:2].reshape(L_SHAPE)
    l2_ref[...] = total[2:].reshape(L_SHAPE)
    r2rows[...] = sum_pair(1, r2sum, r2pair).reshape(32, 128)
    for k in range(4):
        r2_ref[k] = r2rows[pl.ds(k, 8, stride=4), :]

    def finish(c):
        copy_out, copy_in = store(c)
        copy_out.wait()
        copy_in.wait()

    each(NC, finish)
    for n, (_, whole) in enumerate(first + second):
        wait_bytes(whole.at[:, pl.ds(0, N - 1)], ag_send.at[n])
    for n, src in enumerate((s1s, b3s, s3s, bos)):
        wait_bytes(src.at[:, :, pl.ds(0, N - 1)], a2a_send.at[n])
    wait_bytes(lrecv.at[pl.ds(0, NZ - 1)], rs_send.at[0])
    wait_bytes(r2recv.at[pl.ds(0, NZ - 1)], rs_send.at[1])
    wait_bytes(lpair, half_send.at[0])
    wait_bytes(r2pair, half_send.at[1])

    ordered = jnp.zeros((8, 512), F32)
    for q in range(2):
        wait_bytes(r1recv.at[q], rs_recv.at[2 + q])
        total = r1recv[q, 0].astype(F32)
        for d in range(1, N):
            total = total + r1recv[q, d].astype(F32)
        high = total.astype(BF).astype(F32)
        middle = (total - high).astype(BF).astype(F32)
        parts = jnp.concatenate((high, middle, total - high - middle), axis=0).astype(BF)
        moved = mm(parts, perm[pl.ds(256 * q, 256), :])
        ordered = ordered + (moved[:8] + moved[8:16] + moved[16:])
    for k in range(4):
        r1_ref[k] = ordered[:, 128 * k : 128 * k + 128]
    for q in range(2):
        wait_bytes(r1recv.at[q, pl.ds(0, N - 1)], rs_send.at[2 + q])


def settle(*refs):
    sems = refs[12]
    copies = []
    for n in range(6):
        pieces = PIECES if n < 2 else 1
        size = refs[n].shape[0] // pieces
        for p in range(pieces):
            rows = pl.ds(p * size, size)
            copies.append(pltpu.make_async_copy(refs[n].at[rows], refs[6 + n].at[rows], sems.at[n, p]))
    for copy in copies:
        copy.start()
    for copy in copies:
        copy.wait()


def local(activations, cotangent, first_up, second_up, second_down, first_down):
    any_spec = pl.BlockSpec(memory_space=pl.ANY)
    vmem = pl.BlockSpec(memory_space=pltpu.VMEM)
    hbm = pl.BlockSpec(memory_space=pltpu.HBM)
    scratch = [
        pltpu.VMEM((NC, 512, TC), BF),
        pltpu.VMEM((NC, 512, TC), BF),
        pltpu.VMEM((4, N, 8, 128), BF),
        pltpu.VMEM((4, N, 8, 128), BF),
        pltpu.VMEM((2, N) + B_SHAPE[1:], BF),
        pltpu.VMEM((2, N) + B_SHAPE[1:], BF),
        pltpu.VMEM((512, 512), BF),
        pltpu.VMEM((512, 512), BF),
        pltpu.VMEM((512, 512), BF),
        pltpu.VMEM((512, 512), BF),
        pltpu.VMEM((2, 4, 256, 256), BF),
        pltpu.VMEM((2, 4, 256, 256), BF),
        pltpu.VMEM((2, 256, 1024), BF),
        pltpu.VMEM((2, 256, 1024), BF),
        pltpu.VMEM((NC, 2, N, 16, TC), BF),
        pltpu.VMEM((NC, 2, N, 16, TC), BF),
        pltpu.VMEM((NC, 2, N, 16, TC), BF),
        pltpu.VMEM((NC, 2, N, 16, TC), BF),
        pltpu.VMEM((NC, 2, N, 16, TC), BF),
        pltpu.VMEM((NC, 2, N, 16, TC), BF),
        pltpu.VMEM((NC, 2, N, 16, TC), BF),
        pltpu.VMEM((NC, 2, N, 16, TC), BF),
        pltpu.VMEM((2, 2, 1024, TC), BF),
        pltpu.VMEM((2, 2, 1024, TC), F32),
        pltpu.VMEM((1024, TC), BF),
        pltpu.VMEM((512, 512), BF),
        pltpu.VMEM((4, NZ, 2, 16, 256), F32),
        pltpu.VMEM((2, N, 8, 256), F32),
        pltpu.VMEM((2, NZ, 2, 16, 128), F32),
        pltpu.VMEM((2, N, 8, 256), BF),
        pltpu.VMEM((NZ, 4, 2, 16, 256), F32),
        pltpu.VMEM((2, N, 8, 256), BF),
        pltpu.VMEM((NZ, 2, 2, 16, 128), F32),
        pltpu.VMEM((2, 4, 16, 256), F32),
        pltpu.VMEM((2, 2, 16, 128), F32),
        pltpu.VMEM((4, 16, 256), F32),
        pltpu.VMEM((2, 16, 128), F32),
        pltpu.VMEM((32, 128), F32),
        pltpu.SemaphoreType.DMA((4,)),
        pltpu.SemaphoreType.DMA((4,)),
        pltpu.SemaphoreType.DMA((2,)),
        pltpu.SemaphoreType.DMA((4,)),
        pltpu.SemaphoreType.DMA((5, NC)),
        pltpu.SemaphoreType.DMA((4,)),
        pltpu.SemaphoreType.DMA((4,)),
        pltpu.SemaphoreType.DMA((2,)),
        pltpu.SemaphoreType.DMA((2,)),
        pltpu.SemaphoreType.DMA((4,)),
        pltpu.SemaphoreType.DMA((2, NC)),
        pltpu.SemaphoreType.DMA((2, NC)),
    ]
    results = pl.pallas_call(
        kernel,
        name="monarch_layer",
        out_shape=(
            jax.ShapeDtypeStruct((2, N, 16, 2048), BF),
            jax.ShapeDtypeStruct((2, N, 16, 2048), BF),
            jax.ShapeDtypeStruct((4, 8, 128), F32),
            jax.ShapeDtypeStruct(L_SHAPE, F32),
            jax.ShapeDtypeStruct(L_SHAPE, F32),
            jax.ShapeDtypeStruct((4, 8, 128), F32),
        ),
        in_specs=[hbm] * 6,
        out_specs=(any_spec, any_spec, vmem, vmem, vmem, vmem),
        scratch_shapes=scratch,
        compiler_params=pltpu.CompilerParams(
            collective_id=0, has_side_effects=True, vmem_limit_bytes=49 * 1024 * 1024
        ),
    )(
        *(
            pltpu.with_memory_space_constraint(value, pltpu.HBM)
            for value in (
                activations, cotangent, first_up, first_down,
                second_up.reshape(B_SHAPE), second_down.reshape(B_SHAPE),
            )
        )
    )
    results = tuple(r.reshape(512, 2048) for r in results[:2]) + tuple(results[2:])
    return tuple(
        pl.pallas_call(
            settle,
            name="settle",
            out_shape=tuple(jax.ShapeDtypeStruct(r.shape, r.dtype) for r in results),
            in_specs=[any_spec] * 6,
            out_specs=(hbm,) * 6,
            compiler_params=pltpu.CompilerParams(vmem_limit_bytes=1024 * 1024),
            scratch_shapes=[pltpu.SemaphoreType.DMA((6, PIECES))],
        )(*results)
    )


def solution(mesh):
    spec = (P("tensor", "dp"),) * 2 + (P("tensor", "dp", None),) * 4
    return jax.shard_map(local, mesh=mesh, in_specs=spec, out_specs=spec, check_vma=False)
```
